32 devices in a mesh: groups: 2 (over y), st: 4 (over x, core), ch: 4 (over z).
Axes of the slice: x: 2, y: 2, z: 4, core: 2. Of those that a mesh axis runs over, the one named last changes fastest.
Arguments:
- latents: bfloat16 [1280, 1024], P('ch', ('groups', 'st')), parts along dimension 1, may hold values from -6 to 6
- spatial_weight: bfloat16 [9, 1280, 1280], P(None, 'ch'), may hold values from -0.0546875 to 0.0546875
- temporal_weight: bfloat16 [3, 1280, 1280], P(None, 'ch'), may hold values from -0.09375 to 0.09375
- cotangent: bfloat16 [1280, 1024], P('ch', ('groups', 'st')), parts along dimension 1, may hold values from -6 to 6
Outputs:
- temporal_out: bfloat16 [1280, 1024], P('ch', ('groups', 'st')), parts along dimension 1
- latent_grad: bfloat16 [1280, 1024], P('ch', ('groups', 'st')), parts along dimension 1
- spatial_grad: float32 [18, 1280, 1280], P('groups', 'ch', 'st'), parts along dimension 0
- temporal_grad: float32 [6, 1280, 1280], P('groups', 'ch', 'st'), parts along dimension 0
The draws below stay inside these ranges and needn't reach their ends.
There are 2 independent parts, one for each index of `groups`. The reference program is written for one: setup_inputs(seed, part) draws one part's arguments, and reference() takes and returns one part's arrays. A program takes and returns all parts, laid end to end along the dimension named above; an argument that names none is the same for every part. Nothing has to cross between parts.
All inputs are finite; a program needn't handle non-finite values.
Results may differ from the reference program's by a relative error of at most 0.008.
Values may be sent and summed in bfloat16 or wider, within the bound.
No kernel may reach another device: no remote copies, remote signals or barrier semaphores. Data moves between devices by JAX's collectives and lax.ppermute only.
A program may use at most 192 MiB of HBM per device.

```python
import math
import jax
import jax.numpy as jnp
from jax import lax

C = 1280
FT = 2
RT = 2
W = 32
RBANDS = 2
CELLS = 512
N_ST = 4


def steps_of(own_key, dims, split, least, top_value):
    factor_of, own = 1.0, jax.random.fold_in(own_key, 6)
    for dim, blocks in split:
        draws = jnp.exp(jax.random.uniform(jax.random.fold_in(own, dim), (blocks,), jnp.float32, least / len(split), top_value / len(split)))
        factor_of = factor_of * jnp.repeat(draws, dims[dim] // blocks).reshape([-1 if axis == dim else 1 for axis in range(len(dims))])
    return factor_of


def scatter_about(key, shape, scale, most, cuts=(), kind=jnp.bfloat16):
    drawn = jax.random.normal(key, shape, jnp.float32) * scale
    if len(cuts) > 0:
        drawn = steps_of(key, shape, cuts, -0.22, 0.18) * drawn
    return jnp.clip(drawn, min=-most, max=most).astype(kind)


def setup_inputs(seed: int = 0, part: int = 0) -> dict:
    key_list = jax.random.split(jax.random.key(seed), 5)
    own_keys = jax.random.split(jax.random.fold_in(key_list[4], part), 5)
    return {
        "latents": scatter_about(own_keys[0], (C, CELLS), 1.0, 6.0, ((0, 4), (1, 4))),
        "spatial_weight": scatter_about(key_list[1], (9, C, C), (9 * C) ** -0.5, 0.0546875, ((1, 4),)),
        "temporal_weight": scatter_about(key_list[2], (3, C, C), (3 * C) ** -0.5, 0.09375, ((1, 4),)),
        "cotangent": scatter_about(own_keys[3], (C, CELLS), 1.0, 6.0, ((0, 4), (1, 4))),
    }


spatial_offsets = tuple(((0, row_step, col_step) for row_step in (-1, 0, 1) for col_step in (-1, 0, 1)))
temporal_offsets = ((-1, 0, 0), (0, 0, 0), (1, 0, 0))

def to_grid(field):
    frame_blocks = N_ST // RBANDS
    channels = field.shape[0]
    shaped = field.reshape(channels, frame_blocks, RBANDS, FT, RT, W)
    return shaped.transpose(0, 1, 3, 2, 4, 5).reshape(channels, frame_blocks * FT, RBANDS * RT, W)

def to_tiles(field_grid):
    frame_blocks = N_ST // RBANDS
    channels = field_grid.shape[0]
    shaped = field_grid.reshape(channels, frame_blocks, FT, RBANDS, RT, W)
    return shaped.transpose(0, 1, 3, 2, 4, 5).reshape(channels, N_ST * FT * RT * W)

def shifted(field_grid, frame_step, row_step, col_step):
    padded = jnp.pad(field_grid, ((0, 0), (1, 1), (1, 1), (1, 1)))
    channels, frames, row_count, col_count = field_grid.shape
    return lax.slice(padded, (0, 1 + frame_step, 1 + row_step, 1 + col_step), (channels, 1 + frame_step + frames, 1 + row_step + row_count, 1 + col_step + col_count))

def apply_taps(weights, field_grid, offsets, direction, transposed):
    channels = field_grid.shape[0]
    running = jnp.zeros((channels, field_grid[0].size), jnp.float32)
    for position, (frame_step, row_step, col_step) in enumerate(offsets):
        matrix = weights[position].T if transposed else weights[position]
        moved_grid = shifted(field_grid, direction * frame_step, direction * row_step, direction * col_step)
        running = running + jnp.dot(matrix, moved_grid.reshape(channels, -1), preferred_element_type=jnp.float32)
    return running.reshape(field_grid.shape)

def tile_sums(left_grid, right_grid):
    left_tiles = to_tiles(left_grid).reshape(C, N_ST, -1).transpose(1, 0, 2)
    right_tiles = to_tiles(right_grid).reshape(C, N_ST, -1).transpose(1, 0, 2)

    def one_tile(operands):
        partial_sum = jnp.dot(operands[0], operands[1].T, preferred_element_type=jnp.float32).astype(jnp.bfloat16)
        return lax.optimization_barrier(partial_sum).astype(jnp.float32)
    return lax.optimization_barrier(jnp.sum(lax.map(one_tile, (left_tiles, right_tiles)), axis=0))

def reference(latents, spatial_weight, temporal_weight, cotangent):
    latent_grid = to_grid(latents)
    hidden_grid = (latent_grid.astype(jnp.float32) + apply_taps(spatial_weight, latent_grid, spatial_offsets, 1, False)).astype(jnp.bfloat16)
    out_grid = (hidden_grid.astype(jnp.float32) + apply_taps(temporal_weight, hidden_grid, temporal_offsets, 1, False)).astype(jnp.bfloat16)
    upstream_grid = to_grid(cotangent)
    hidden_grad = (upstream_grid.astype(jnp.float32) + apply_taps(temporal_weight, upstream_grid, temporal_offsets, -1, True)).astype(jnp.bfloat16)
    latent_grad = (hidden_grad.astype(jnp.float32) + apply_taps(spatial_weight, hidden_grad, spatial_offsets, -1, True)).astype(jnp.bfloat16)
    grad_scale = 1.0 / math.sqrt(CELLS)
    temporal_grad = jnp.stack([tile_sums(upstream_grid, shifted(hidden_grid, offset_set[0], offset_set[1], offset_set[2])) for offset_set in temporal_offsets]) * grad_scale
    spatial_grad = jnp.stack([tile_sums(hidden_grad, shifted(latent_grid, offset_set[0], offset_set[1], offset_set[2])) for offset_set in spatial_offsets]) * grad_scale
    return (to_tiles(out_grid), to_tiles(latent_grad), spatial_grad, temporal_grad)
```

```python
import math

import jax
import jax.numpy as jnp
from jax import lax
from jax.experimental import pallas as pl
from jax.experimental.pallas import tpu as pltpu
from jax.sharding import PartitionSpec as P

FT = 2
RT = 2
W = 32
RBANDS = 2
TILE = FT * RT * W
HALF = RT * W
ROWS = RBANDS * RT
FRAME = ROWS * W
MIB = 1 << 20
BF = jnp.bfloat16
F32 = jnp.float32


def sizes():
    return lax.axis_size("ch"), lax.axis_size("st") // RBANDS


def place():
    st = lax.axis_index("st")
    return lax.axis_index("ch"), st // RBANDS, st % RBANDS


def send(data, axis, by):
    n = lax.axis_size(axis)
    return lax.ppermute(data, axis, [(i, (i + by) % n) for i in range(n)])


def swap_band(data):
    n = lax.axis_size("st")
    return lax.ppermute(data, "st", [(i, i ^ 1) for i in range(n)])


def gather_ch(shard):
    n_ch, _ = sizes()
    return jnp.stack([shard] + [send(shard, "ch", k) for k in range(1, n_ch)])


def ring_blocks(data):
    _, n_x = sizes()
    return [send(data, "st", RBANDS * j) for j in range(1, n_x)]


def neighbours(data):
    _, n_x = sizes()
    if n_x == 2:
        other = send(data, "st", RBANDS)
        return other, other
    return send(data, "st", RBANDS), send(data, "st", -RBANDS)


def lanes(shape):
    return lax.broadcasted_iota(jnp.int32, shape, len(shape) - 1)


def roll(x, by):
    return pltpu.roll(x, by, x.ndim - 1)


def frames_of(own, sibling, band):
    own = own.astype(F32)
    sibling = sibling.astype(F32)
    first = jnp.where(band == 0, own, sibling)
    second = jnp.where(band == 0, sibling, own)
    low = lanes(first.shape) < HALF
    return jnp.where(low, first, roll(second, HALF)), jnp.where(low, roll(first, HALF), second)


def tile_of(frame0, frame1, band):
    low = lanes(frame0.shape) < HALF
    upper = jnp.where(low, frame0, roll(frame1, HALF))
    lower = jnp.where(low, roll(frame0, HALF), frame1)
    return jnp.where(band == 0, upper, lower)


def time_pieces(own, before, after, m, n_x):
    own32 = own.astype(F32)
    before = jnp.where(m > 0, before.astype(F32), 0.0)
    after = jnp.where(m < n_x - 1, after.astype(F32), 0.0)
    low = lanes(own32.shape) < HALF
    earlier = roll(jnp.where(low, own32, before), HALF)
    later = roll(jnp.where(low, after, own32), HALF)
    return earlier.astype(BF), own, later.astype(BF)


def inside(dr, dc, shape):
    lane = lanes(shape)
    row = lane // W + dr
    col = lane % W + dc
    return (row >= 0) & (row < ROWS) & (col >= 0) & (col < W)


def spatial_forward(latents, mine, sibling, weight):
    n_ch, n_x = sizes()
    cb = latents.shape[0]
    channels = n_ch * cb

    def body(latents_ref, mine_ref, sibling_ref, w_ref, out_ref, field, acc):
        c, _, band = place()
        tap = pl.program_id(0)

        @pl.when(tap == 0)
        def _():
            for k in range(n_ch):
                at = pl.ds(pl.multiple_of(((c + n_ch - k) % n_ch) * cb, 16), cb)
                f0, f1 = frames_of(mine_ref[k], sibling_ref[k], band)
                field[at, :FRAME] = f0.astype(BF)
                field[at, FRAME:] = f1.astype(BF)
            acc[...] = jnp.zeros_like(acc)

        dr = tap // 3 - 1
        dc = tap % 3 - 1
        part = jnp.dot(w_ref[0], field[...], preferred_element_type=F32)
        by = (FRAME - (W * dr + dc)) % FRAME
        ok = inside(dr, dc, (cb, FRAME))
        acc[:, :FRAME] += jnp.where(ok, roll(part[:, :FRAME], by), 0.0)
        acc[:, FRAME:] += jnp.where(ok, roll(part[:, FRAME:], by), 0.0)

        @pl.when(tap == 8)
        def _():
            total = tile_of(acc[:, :FRAME], acc[:, FRAME:], band)
            out_ref[...] = (latents_ref[...].astype(F32) + total).astype(BF)

    whole = lambda shape: pl.BlockSpec(shape, lambda g: (0,) * len(shape))
    return pl.pallas_call(
        body,
        grid=(9,),
        in_specs=[
            whole((cb, TILE)),
            whole((n_ch, cb, TILE)),
            whole((n_ch, cb, TILE)),
            pl.BlockSpec((1, cb, channels), lambda g: (g, 0, 0)),
        ],
        out_specs=whole((cb, TILE)),
        out_shape=jax.ShapeDtypeStruct((cb, TILE), BF),
        scratch_shapes=[pltpu.VMEM((channels, 2 * FRAME), BF), pltpu.VMEM((cb, 2 * FRAME), F32)],
        compiler_params=pltpu.CompilerParams(vmem_limit_bytes=16 * MIB),
        name="spatial_forward",
    )(latents, mine, sibling, weight)


def temporal_forward(hidden, mine, before, after, weight):
    n_ch, n_x = sizes()
    cb = hidden.shape[0]
    channels = n_ch * cb

    def body(hidden_ref, mine_ref, before_ref, after_ref, w_ref, out_ref, field):
        c, m, _ = place()
        for k in range(n_ch):
            at = pl.ds(pl.multiple_of(((c + n_ch - k) % n_ch) * cb, 16), cb)
            pieces = time_pieces(mine_ref[k], before_ref[k], after_ref[k], m, n_x)
            for d in range(3):
                field[d, at, :] = pieces[d]
        total = hidden_ref[...].astype(F32)
        for d in range(3):
            total += jnp.dot(w_ref[d], field[d], preferred_element_type=F32)
        out_ref[...] = total.astype(BF)

    return pl.pallas_call(
        body,
        out_shape=jax.ShapeDtypeStruct((cb, TILE), BF),
        scratch_shapes=[pltpu.VMEM((3, channels, TILE), BF)],
        compiler_params=pltpu.CompilerParams(vmem_limit_bytes=16 * MIB),
        name="temporal_forward",
    )(hidden, mine, before, after, weight)


def emit_chunks(total, scratch, out_refs, c, n_ch, cb):
    scratch[...] = total.T
    for k in range(n_ch):
        at = pl.ds(pl.multiple_of(((c + k) % n_ch) * cb, 16), cb)
        out_refs[k][...] = scratch[at, :].astype(out_refs[k].dtype)


def chunk_shapes(n_ch, cb):
    return [jax.ShapeDtypeStruct((cb, TILE), BF if k else F32) for k in range(n_ch)]


def temporal_backward(field, before, after, weight):
    n_ch, n_x = sizes()
    cb = field.shape[0]
    channels = n_ch * cb

    def body(field_ref, before_ref, after_ref, w_ref, *rest):
        out_refs, scratch = rest[:n_ch], rest[n_ch]
        c, m, _ = place()
        pieces = time_pieces(field_ref[...], before_ref[...], after_ref[...], m, n_x)
        total = jnp.zeros((TILE, channels), F32)
        for d in range(3):
            left = pieces[2 - d].astype(F32).T.astype(BF)
            total += jnp.dot(left, w_ref[d], preferred_element_type=F32)
        emit_chunks(total, scratch, out_refs, c, n_ch, cb)

    return pl.pallas_call(
        body,
        out_shape=chunk_shapes(n_ch, cb),
        scratch_shapes=[pltpu.VMEM((channels, TILE), F32)],
        compiler_params=pltpu.CompilerParams(vmem_limit_bytes=16 * MIB),
        name="temporal_backward",
    )(field, before, after, weight)


def spatial_backward(field, sibling, weight):
    n_ch, _ = sizes()
    cb = field.shape[0]
    channels = n_ch * cb

    def body(field_ref, sibling_ref, w_ref, *rest):
        out_refs, (left, acc, scratch) = rest[:n_ch], rest[n_ch:]
        c, _, band = place()
        step = pl.program_id(0)

        @pl.when(step == 0)
        def _():
            f0, f1 = frames_of(field_ref[...], sibling_ref[...], band)
            left[...] = jnp.zeros_like(left)
            col = lax.broadcasted_iota(jnp.int32, (FRAME, cb), 0) % W
            for a, frame in enumerate((f0, f1)):
                cells = frame.T
                for q in range(3):
                    dc = q - 1
                    moved = pltpu.roll(cells, dc % FRAME, 0) if dc else cells
                    ok = (col - dc >= 0) & (col - dc < W)
                    left[a, W : W + FRAME, q * cb : (q + 1) * cb] = jnp.where(ok, moved, 0.0).astype(BF)
            acc[...] = jnp.zeros_like(acc)

        start = pl.multiple_of(W + HALF * band - W * (step - 1), W)
        rows = jnp.concatenate([left[0, pl.ds(start, HALF), :], left[1, pl.ds(start, HALF), :]], axis=0)
        acc[...] += jnp.dot(rows, w_ref[...], preferred_element_type=F32)

        @pl.when(step == 2)
        def _():
            emit_chunks(acc[...], scratch, out_refs, c, n_ch, cb)

    whole = lambda shape: pl.BlockSpec(shape, lambda g: (0,) * len(shape))
    return pl.pallas_call(
        body,
        grid=(3,),
        in_specs=[
            whole((cb, TILE)),
            whole((cb, TILE)),
            pl.BlockSpec((3 * cb, channels), lambda g: (g, 0)),
        ],
        out_specs=[whole((cb, TILE)) for _ in range(n_ch)],
        out_shape=chunk_shapes(n_ch, cb),
        scratch_shapes=[
            pltpu.VMEM((2, FRAME + 2 * W, 3 * cb), BF),
            pltpu.VMEM((TILE, channels), F32),
            pltpu.VMEM((channels, TILE), F32),
        ],
        compiler_params=pltpu.CompilerParams(vmem_limit_bytes=24 * MIB),
        name="spatial_backward",
    )(field, sibling, weight.reshape(9 * cb, channels))


def contract_cells(a, b):
    return lax.dot_general(a, b, (((1,), (1,)), ((), ())), preferred_element_type=F32)


def spatial_grads(grads, grads_sibling, fields, fields_sibling, scale):
    n_x, ob, _ = grads.shape
    ib = fields.shape[1]

    def body(g_ref, gs_ref, l_ref, ls_ref, out_ref, left, right):
        _, _, band = place()
        tap = pl.program_id(0)

        @pl.when(tap == 0)
        def _():
            for j in range(n_x):
                for a, frame in enumerate(frames_of(g_ref[j], gs_ref[j], band)):
                    left[:, (2 * j + a) * FRAME : (2 * j + a + 1) * FRAME] = frame.astype(BF)
                for a, frame in enumerate(frames_of(l_ref[j], ls_ref[j], band)):
                    right[2 * j + a] = frame

        dr = tap // 3 - 1
        dc = tap % 3 - 1
        by = (FRAME - (W * dr + dc)) % FRAME
        ok = inside(dr, dc, (ib, FRAME))
        moved = [jnp.where(ok, roll(right[f], by), 0.0).astype(BF) for f in range(2 * n_x)]
        out_ref[0] = contract_cells(left[...], jnp.concatenate(moved, axis=1)) * scale

    whole = lambda shape: pl.BlockSpec(shape, lambda g: (0,) * len(shape))
    return pl.pallas_call(
        body,
        grid=(9,),
        in_specs=[whole((n_x, ob, TILE))] * 2 + [whole((n_x, ib, TILE))] * 2,
        out_specs=pl.BlockSpec((1, ob, ib), lambda g: (g, 0, 0)),
        out_shape=jax.ShapeDtypeStruct((9, ob, ib), F32),
        scratch_shapes=[pltpu.VMEM((ob, 2 * n_x * FRAME), BF), pltpu.VMEM((2 * n_x, ib, FRAME), F32)],
        compiler_params=pltpu.CompilerParams(vmem_limit_bytes=24 * MIB),
        name="spatial_grads",
    )(grads, grads_sibling, fields, fields_sibling)


def temporal_grads(grads, grads_sibling, fields, fields_sibling, scale):
    n_x, ob, _ = grads.shape
    ib = fields.shape[1]
    span = 2 * n_x * FRAME

    def body(g_ref, gs_ref, h_ref, hs_ref, out_ref, left, right):
        _, m, band = place()
        step = pl.program_id(0)

        @pl.when(step == 0)
        def _():
            right[:, :FRAME] = jnp.zeros((ib, FRAME), BF)
            right[:, FRAME + span :] = jnp.zeros((ib, FRAME), BF)
            for j in range(n_x):
                block = (m + n_x - j) % n_x
                for a, frame in enumerate(frames_of(g_ref[j], gs_ref[j], band)):
                    at = pl.multiple_of((2 * block + a) * FRAME, FRAME)
                    left[:, pl.ds(at, FRAME)] = frame.astype(BF)
                for a, frame in enumerate(frames_of(h_ref[j], hs_ref[j], band)):
                    at = pl.multiple_of((2 * block + a + 1) * FRAME, FRAME)
                    right[:, pl.ds(at, FRAME)] = frame.astype(BF)

        moved = right[:, pl.ds(pl.multiple_of(step * FRAME, FRAME), span)]
        out_ref[0] = contract_cells(left[...], moved) * scale

    whole = lambda shape: pl.BlockSpec(shape, lambda g: (0,) * len(shape))
    return pl.pallas_call(
        body,
        grid=(3,),
        in_specs=[whole((n_x, ob, TILE))] * 2 + [whole((n_x, ib, TILE))] * 2,
        out_specs=pl.BlockSpec((1, ob, ib), lambda g: (g, 0, 0)),
        out_shape=jax.ShapeDtypeStruct((3, ob, ib), F32),
        scratch_shapes=[pltpu.VMEM((ob, span), BF), pltpu.VMEM((ib, span + 2 * FRAME), BF)],
        compiler_params=pltpu.CompilerParams(vmem_limit_bytes=24 * MIB),
        name="temporal_grads",
    )(grads, grads_sibling, fields, fields_sibling)


def reduce_ch(base, chunks):
    total = base.astype(F32) + chunks[0]
    for k in range(1, len(chunks)):
        total = total + send(chunks[k], "ch", k).astype(F32)
    return total.astype(BF)


def on_device(latents, spatial_weight, temporal_weight, cotangent):
    n_ch, n_x = sizes()
    assert n_ch == RBANDS * n_x
    c, m, band = place()
    scale = 1.0 / math.sqrt(TILE * RBANDS * n_x)

    def block(stack, b):
        return lax.dynamic_index_in_dim(stack, (c + n_ch - b) % n_ch, 0, keepdims=False)

    mine = gather_ch(latents)
    sibling = swap_band(mine)
    hidden = spatial_forward(latents, mine, sibling, spatial_weight)

    cot_ring = ring_blocks(cotangent)
    if n_x == 2:
        cot_before = cot_after = cot_ring[0]
    else:
        cot_before, cot_after = cot_ring[0], cot_ring[-1]
    hidden_grad = reduce_ch(
        cotangent, temporal_backward(cotangent, cot_before, cot_after, temporal_weight)
    )
    grad_sibling = swap_band(hidden_grad)
    latent_grad = reduce_ch(
        hidden_grad, spatial_backward(hidden_grad, grad_sibling, spatial_weight)
    )

    hidden_mine = gather_ch(hidden)
    before, after = neighbours(hidden_mine)
    temporal_out = temporal_forward(hidden, hidden_mine, before, after, temporal_weight)

    own_block = RBANDS * m + band
    sib_block = RBANDS * m + 1 - band

    cots = jnp.stack([cotangent] + cot_ring)
    cots_sibling = swap_band(cots)

    hid_own, hid_sib = [block(hidden_mine, own_block)], [block(hidden_mine, sib_block)]
    for j in range(1, n_x):
        if n_x == 2:
            hid_own.append(block(before, own_block))
            hid_sib.append(block(before, sib_block))
        else:
            target = RBANDS * ((m + j) % n_x)
            both = jnp.stack([block(hidden_mine, target + band), block(hidden_mine, target + 1 - band)])
            both = send(both, "st", RBANDS * j)
            hid_own.append(both[0])
            hid_sib.append(both[1])
    hids = jnp.stack(hid_own)
    hids_sibling = swap_band(jnp.stack(hid_sib))
    temporal_grad = temporal_grads(cots, cots_sibling, hids, hids_sibling, scale)

    lat_own, lat_sib = [block(mine, own_block)], [block(sibling, own_block)]
    grad_own, grad_sib = [hidden_grad], [grad_sibling]
    for j in range(1, n_x):
        target = RBANDS * ((m + j) % n_x) + band
        both = send(jnp.stack([block(mine, target), block(sibling, target)]), "st", RBANDS * j)
        lat_own.append(both[0])
        lat_sib.append(both[1])
        both = send(jnp.stack([hidden_grad, grad_sibling]), "st", RBANDS * j)
        grad_own.append(both[0])
        grad_sib.append(both[1])
    spatial_grad = spatial_grads(
        jnp.stack(grad_own), jnp.stack(grad_sib), jnp.stack(lat_own), jnp.stack(lat_sib), scale
    )
    return temporal_out, latent_grad, spatial_grad, temporal_grad


def solution(mesh):
    return jax.shard_map(
        on_device,
        mesh=mesh,
        in_specs=(
            P("ch", ("groups", "st")),
            P(None, "ch", None),
            P(None, "ch", None),
            P("ch", ("groups", "st")),
        ),
        out_specs=(
            P("ch", ("groups", "st")),
            P("ch", ("groups", "st")),
            P("groups", "ch", "st"),
            P("groups", "ch", "st"),
        ),
        check_vma=False,
    )
```

```python
import math

import jax
import jax.numpy as jnp
from jax import lax
from jax.experimental import pallas as pl
from jax.experimental.pallas import tpu as pltpu
from jax.sharding import PartitionSpec as P

FT = 2
RT = 2
W = 32
RBANDS = 2
TILE = FT * RT * W
HALF = RT * W
ROWS = RBANDS * RT
FRAME = ROWS * W
MIB = 1 << 20
BF = jnp.bfloat16
F32 = jnp.float32


def sizes():
    return lax.axis_size("ch"), lax.axis_size("st") // RBANDS


def place():
    st = lax.axis_index("st")
    return lax.axis_index("ch"), st // RBANDS, st % RBANDS


def send(data, axis, by):
    n = lax.axis_size(axis)
    return lax.ppermute(data, axis, [(i, (i + by) % n) for i in range(n)])


def swap_band(data):
    n = lax.axis_size("st")
    return lax.ppermute(data, "st", [(i, i ^ 1) for i in range(n)])


def gather_ch(shard):
    n_ch, _ = sizes()
    return [shard] + [send(shard, "ch", k) for k in range(1, n_ch)]


def ring_blocks(data):
    _, n_x = sizes()
    return [send(data, "st", RBANDS * j) for j in range(1, n_x)]


def neighbours(data):
    _, n_x = sizes()
    if n_x == 2:
        other = send(data, "st", RBANDS)
        return other, other
    return send(data, "st", RBANDS), send(data, "st", -RBANDS)


def lanes(shape):
    return lax.broadcasted_iota(jnp.int32, shape, len(shape) - 1)


def roll(x, by):
    return pltpu.roll(x, by, x.ndim - 1)


def frames_of(own, sibling, band):
    own = own.astype(F32)
    sibling = sibling.astype(F32)
    first = jnp.where(band == 0, own, sibling)
    second = jnp.where(band == 0, sibling, own)
    low = lanes(first.shape) < HALF
    return jnp.where(low, first, roll(second, HALF)), jnp.where(low, roll(first, HALF), second)


def tile_of(frame0, frame1, band):
    low = lanes(frame0.shape) < HALF
    upper = jnp.where(low, frame0, roll(frame1, HALF))
    lower = jnp.where(low, roll(frame0, HALF), frame1)
    return jnp.where(band == 0, upper, lower)


def time_pieces(own, before, after, m, n_x):
    own32 = own.astype(F32)
    before = jnp.where(m > 0, before.astype(F32), 0.0)
    after = jnp.where(m < n_x - 1, after.astype(F32), 0.0)
    low = lanes(own32.shape) < HALF
    earlier = roll(jnp.where(low, own32, before), HALF)
    later = roll(jnp.where(low, after, own32), HALF)
    return earlier.astype(BF), own, later.astype(BF)


def inside(dr, dc, shape):
    lane = lanes(shape)
    row = lane // W + dr
    col = lane % W + dc
    return (row >= 0) & (row < ROWS) & (col >= 0) & (col < W)


def spatial_forward(mine, siblings, weight):
    n_ch, n_x = sizes()
    cb = mine[0].shape[0]
    channels = n_ch * cb

    def body(*refs):
        mine_refs, sibling_refs = refs[:n_ch], refs[n_ch : 2 * n_ch]
        w_ref, out_ref, field, acc = refs[2 * n_ch :]
        c, _, band = place()
        for k in range(n_ch):
            at = pl.ds(pl.multiple_of(((c + n_ch - k) % n_ch) * cb, 16), cb)
            f0, f1 = frames_of(mine_refs[k][...], sibling_refs[k][...], band)
            field[at, :FRAME] = f0.astype(BF)
            field[at, FRAME:] = f1.astype(BF)
        for tap in range(9):
            dr, dc = tap // 3 - 1, tap % 3 - 1
            part = jnp.dot(w_ref[tap], field[...], preferred_element_type=F32)
            by = (-(W * dr + dc)) % FRAME
            ok = inside(dr, dc, (cb, FRAME))
            for a in range(FT):
                at = slice(a * FRAME, (a + 1) * FRAME)
                moved = part[:, at]
                if by:
                    moved = jnp.where(ok, roll(moved, by), 0.0)
                acc[:, at] = moved + acc[:, at] if tap else moved
        total = tile_of(acc[:, :FRAME], acc[:, FRAME:], band)
        out_ref[...] = (mine_refs[0][...].astype(F32) + total).astype(BF)

    return pl.pallas_call(
        body,
        out_shape=jax.ShapeDtypeStruct((cb, TILE), BF),
        scratch_shapes=[pltpu.VMEM((channels, FT * FRAME), BF), pltpu.VMEM((cb, FT * FRAME), F32)],
        compiler_params=pltpu.CompilerParams(vmem_limit_bytes=16 * MIB),
        name="spatial_forward",
    )(*mine, *siblings, weight)


def temporal_forward(mine, before, after, weight):
    n_ch, n_x = sizes()
    cb = mine[0].shape[0]
    channels = n_ch * cb

    def body(*refs):
        mine_refs = refs[:n_ch]
        before_ref, after_ref, w_ref, out_ref, field = refs[n_ch:]
        c, m, _ = place()
        for k in range(n_ch):
            at = pl.ds(pl.multiple_of(((c + n_ch - k) % n_ch) * cb, 16), cb)
            pieces = time_pieces(mine_refs[k][...], before_ref[k], after_ref[k], m, n_x)
            for d in range(3):
                field[d, at, :] = pieces[d]
        total = mine_refs[0][...].astype(F32)
        for d in range(3):
            total += jnp.dot(w_ref[d], field[d], preferred_element_type=F32)
        out_ref[...] = total.astype(BF)

    return pl.pallas_call(
        body,
        out_shape=jax.ShapeDtypeStruct((cb, TILE), BF),
        scratch_shapes=[pltpu.VMEM((3, channels, TILE), BF)],
        compiler_params=pltpu.CompilerParams(vmem_limit_bytes=16 * MIB),
        name="temporal_forward",
    )(*mine, before, after, weight)


def emit_chunks(total, scratch, out_refs, c, n_ch, cb):
    scratch[...] = total.T
    for k in range(n_ch):
        at = pl.ds(pl.multiple_of(((c + k) % n_ch) * cb, 16), cb)
        out_refs[k][...] = scratch[at, :].astype(out_refs[k].dtype)


def chunk_shapes(n_ch, cb):
    return [jax.ShapeDtypeStruct((cb, TILE), BF if k else F32) for k in range(n_ch)]


def temporal_backward(field, before, after, weight):
    n_ch, n_x = sizes()
    cb = field.shape[0]
    channels = n_ch * cb

    def body(field_ref, before_ref, after_ref, w_ref, *rest):
        out_refs, scratch = rest[:n_ch], rest[n_ch]
        c, m, _ = place()
        pieces = time_pieces(field_ref[...], before_ref[...], after_ref[...], m, n_x)
        total = jnp.zeros((TILE, channels), F32)
        for d in range(3):
            left = pieces[2 - d].astype(F32).T.astype(BF)
            total += jnp.dot(left, w_ref[d], preferred_element_type=F32)
        emit_chunks(total, scratch, out_refs, c, n_ch, cb)

    return pl.pallas_call(
        body,
        out_shape=chunk_shapes(n_ch, cb),
        scratch_shapes=[pltpu.VMEM((channels, TILE), F32)],
        compiler_params=pltpu.CompilerParams(vmem_limit_bytes=16 * MIB),
        name="temporal_backward",
    )(field, before, after, weight)


def shifted_columns(frame, toward):
    cells = frame.T
    col = lax.broadcasted_iota(jnp.int32, cells.shape, 0) % W
    out = []
    for dc in (-toward, 0, toward):
        moved = cells
        if dc:
            ok = (col + dc >= 0) & (col + dc < W)
            moved = jnp.where(ok, pltpu.roll(cells, (-dc) % FRAME, 0), 0.0)
        out.append(moved.astype(BF))
    return out


def spatial_backward(field, sibling, weight):
    n_ch, _ = sizes()
    cb = field.shape[0]
    channels = n_ch * cb

    def body(field_ref, sibling_ref, w_ref, *rest):
        out_refs, (left, scratch) = rest[:n_ch], rest[n_ch:]
        c, _, band = place()
        blank = jnp.zeros((W, 3 * cb), BF)
        for a, frame in enumerate(frames_of(field_ref[...], sibling_ref[...], band)):
            left[a, :W, :] = blank
            left[a, W + FRAME :, :] = blank
            for q, moved in enumerate(shifted_columns(frame, -1)):
                left[a, W : W + FRAME, q * cb : (q + 1) * cb] = moved
        total = jnp.zeros((TILE, channels), F32)
        for g in range(3):
            start = pl.multiple_of(HALF * band + W * (2 - g), W)
            rows = jnp.concatenate([left[a, pl.ds(start, HALF), :] for a in range(FT)], axis=0)
            total += jnp.dot(rows, w_ref[g], preferred_element_type=F32)
        emit_chunks(total, scratch, out_refs, c, n_ch, cb)

    return pl.pallas_call(
        body,
        out_shape=chunk_shapes(n_ch, cb),
        scratch_shapes=[
            pltpu.VMEM((FT, FRAME + 2 * W, 3 * cb), BF),
            pltpu.VMEM((channels, TILE), F32),
        ],
        compiler_params=pltpu.CompilerParams(vmem_limit_bytes=16 * MIB),
        name="spatial_backward",
    )(field, sibling, weight.reshape(3, 3 * cb, channels))


def pairs_from(own, sibling, rest):
    return [(own, sibling)] + [(both.at[0], both.at[1]) for both in rest]


def spatial_grads(grads, fields, scale):
    _, n_x = sizes()
    ob, ib = grads[0].shape[0], fields[0].shape[0]
    frames = FT * n_x
    n_in = n_x + 1

    def body(*refs):
        g_refs, l_refs = refs[:n_in], refs[n_in : 2 * n_in]
        out_ref, left, right = refs[2 * n_in :]
        _, _, band = place()
        step = pl.program_id(0)

        @pl.when(step == 0)
        def _():
            blank = jnp.zeros((W, ib), BF)
            g_pairs = pairs_from(g_refs[0], g_refs[1], g_refs[2:])
            l_pairs = pairs_from(l_refs[0], l_refs[1], l_refs[2:])
            for j in range(n_x):
                for a, frame in enumerate(frames_of(g_pairs[j][0][...], g_pairs[j][1][...], band)):
                    f = FT * j + a
                    left[:, f * FRAME : (f + 1) * FRAME] = frame.astype(BF)
                for a, frame in enumerate(frames_of(l_pairs[j][0][...], l_pairs[j][1][...], band)):
                    f = FT * j + a
                    for q, moved in enumerate(shifted_columns(frame, 1)):
                        right[q, f, :W, :] = blank
                        right[q, f, W + FRAME :, :] = blank
                        right[q, f, W : W + FRAME, :] = moved

        start = pl.multiple_of(W * (step // 3), W)
        moved = jnp.concatenate([right[step % 3, f, pl.ds(start, FRAME), :] for f in range(frames)], axis=0)
        out_ref[0] = jnp.dot(left[...], moved, preferred_element_type=F32) * scale

    whole = lambda x: pl.BlockSpec(x.shape, lambda g: (0,) * x.ndim)
    args = (*grads[:2], *grads[2], *fields[:2], *fields[2])
    return pl.pallas_call(
        body,
        grid=(9,),
        in_specs=[whole(x) for x in args],
        out_specs=pl.BlockSpec((1, ob, ib), lambda g: (g, 0, 0)),
        out_shape=jax.ShapeDtypeStruct((9, ob, ib), F32),
        scratch_shapes=[
            pltpu.VMEM((ob, frames * FRAME), BF),
            pltpu.VMEM((3, frames, FRAME + 2 * W, ib), BF),
        ],
        compiler_params=pltpu.CompilerParams(vmem_limit_bytes=24 * MIB),
        name="spatial_grads",
    )(*args)


def temporal_grads(grads, grads_sibling, fields, fields_sibling, scale):
    _, n_x = sizes()
    ob, ib = grads[0].shape[0], fields[0].shape[0]
    span = FT * n_x * FRAME

    def body(*refs):
        g_refs, gs_refs, h_refs, hs_refs = (refs[q * n_x : (q + 1) * n_x] for q in range(4))
        out_ref, left, right = refs[4 * n_x :]
        _, m, band = place()
        right[:FRAME, :] = jnp.zeros((FRAME, ib), BF)
        right[FRAME + span :, :] = jnp.zeros((FRAME, ib), BF)
        for j in range(n_x):
            block = (m + n_x - j) % n_x
            for a, frame in enumerate(frames_of(g_refs[j][...], gs_refs[j][...], band)):
                at = pl.multiple_of((FT * block + a) * FRAME, FRAME)
                left[:, pl.ds(at, FRAME)] = frame.astype(BF)
            for a, frame in enumerate(frames_of(h_refs[j][...], hs_refs[j][...], band)):
                at = pl.multiple_of((FT * block + a + 1) * FRAME, FRAME)
                right[pl.ds(at, FRAME), :] = frame.T.astype(BF)
        for d in range(3):
            moved = right[d * FRAME : d * FRAME + span, :]
            out_ref[d] = jnp.dot(left[...], moved, preferred_element_type=F32) * scale

    return pl.pallas_call(
        body,
        out_shape=jax.ShapeDtypeStruct((3, ob, ib), F32),
        scratch_shapes=[pltpu.VMEM((ob, span), BF), pltpu.VMEM((span + 2 * FRAME, ib), BF)],
        compiler_params=pltpu.CompilerParams(vmem_limit_bytes=24 * MIB),
        name="temporal_grads",
    )(*grads, *grads_sibling, *fields, *fields_sibling)


def reduce_ch(base, chunks):
    total = base.astype(F32) + chunks[0]
    for k in range(1, len(chunks)):
        total = total + send(chunks[k], "ch", k).astype(F32)
    return total.astype(BF)


def on_device(latents, spatial_weight, temporal_weight, cotangent):
    n_ch, n_x = sizes()
    assert n_ch == RBANDS * n_x
    c, m, band = place()
    scale = 1.0 / math.sqrt(TILE * RBANDS * n_x)

    def block(pieces, b):
        stack = jnp.stack(pieces) if isinstance(pieces, list) else pieces
        return lax.dynamic_index_in_dim(stack, (c + n_ch - b) % n_ch, 0, keepdims=False)

    cot_ring = ring_blocks(cotangent)
    mine = gather_ch(latents)
    chunks = temporal_backward(cotangent, cot_ring[0], cot_ring[-1], temporal_weight)

    siblings = [swap_band(piece) for piece in mine]
    hidden = spatial_forward(mine, siblings, spatial_weight)
    hidden, base = lax.optimization_barrier((hidden, cotangent))

    hidden_grad = reduce_ch(base, chunks)
    grad_sibling = swap_band(hidden_grad)
    chunks = spatial_backward(hidden_grad, grad_sibling, spatial_weight)
    latent_grad = reduce_ch(hidden_grad, chunks)

    hidden_mine = gather_ch(hidden)
    before, after = neighbours(jnp.stack(hidden_mine))
    temporal_out = temporal_forward(hidden_mine, before, after, temporal_weight)

    own_block = RBANDS * m + band
    sib_block = RBANDS * m + 1 - band

    hid_own, hid_sib = [block(hidden_mine, own_block)], [block(hidden_mine, sib_block)]
    for j in range(1, n_x):
        if n_x == 2:
            hid_own.append(block(before, own_block))
            hid_sib.append(block(before, sib_block))
        else:
            target = RBANDS * ((m + j) % n_x)
            both = jnp.stack([block(hidden_mine, target + band), block(hidden_mine, target + 1 - band)])
            both = send(both, "st", RBANDS * j)
            hid_own.append(both[0])
            hid_sib.append(both[1])
    cots = [cotangent] + cot_ring
    temporal_grad = temporal_grads(
        cots, [swap_band(x) for x in cots], hid_own, [swap_band(x) for x in hid_sib], scale
    )

    lat_rest, grad_rest = [], []
    for j in range(1, n_x):
        target = RBANDS * ((m + j) % n_x) + band
        both = jnp.stack([block(mine, target), block(siblings, target)])
        lat_rest.append(send(both, "st", RBANDS * j))
        grad_rest.append(send(jnp.stack([hidden_grad, grad_sibling]), "st", RBANDS * j))
    spatial_grad = spatial_grads(
        (hidden_grad, grad_sibling, grad_rest),
        (block(mine, own_block), block(siblings, own_block), lat_rest),
        scale,
    )
    return temporal_out, latent_grad, spatial_grad, temporal_grad


def solution(mesh):
    return jax.shard_map(
        on_device,
        mesh=mesh,
        in_specs=(
            P("ch", ("groups", "st")),
            P(None, "ch", None),
            P(None, "ch", None),
            P("ch", ("groups", "st")),
        ),
        out_specs=(
            P("ch", ("groups", "st")),
            P("ch", ("groups", "st")),
            P("groups", "ch", "st"),
            P("groups", "ch", "st"),
        ),
        check_vma=False,
    )
```

```python
import math

import jax
import jax.numpy as jnp
from jax import lax
from jax.experimental import pallas as pl
from jax.experimental.pallas import tpu as pltpu
from jax.sharding import PartitionSpec as P

FT = 2
RT = 2
W = 32
RBANDS = 2
TILE = FT * RT * W
HALF = RT * W
ROWS = RBANDS * RT
FRAME = ROWS * W
MIB = 1 << 20
BF = jnp.bfloat16
F32 = jnp.float32


def sizes():
    return lax.axis_size("ch"), lax.axis_size("st") // RBANDS


def place():
    st = lax.axis_index("st")
    return lax.axis_index("ch"), st // RBANDS, st % RBANDS


def send(data, axis, by):
    n = lax.axis_size(axis)
    return lax.ppermute(data, axis, [(i, (i + by) % n) for i in range(n)])


def swap_band(data):
    n = lax.axis_size("st")
    return lax.ppermute(data, "st", [(i, i ^ 1) for i in range(n)])


def after_all(values, others):
    return lax.optimization_barrier((values, others))[0]


def gather_ch(shard):
    n_ch, _ = sizes()
    return [shard] + [send(shard, "ch", k) for k in range(1, n_ch)]


def ring_blocks(data):
    _, n_x = sizes()
    return [send(data, "st", RBANDS * j) for j in range(1, n_x)]


def neighbours(data):
    _, n_x = sizes()
    if n_x == 2:
        other = send(data, "st", RBANDS)
        return other, other
    return send(data, "st", RBANDS), send(data, "st", -RBANDS)


def lanes(shape):
    return lax.broadcasted_iota(jnp.int32, shape, len(shape) - 1)


def roll(x, by):
    return pltpu.roll(x, by, x.ndim - 1)


def frames_of(own, sibling, band):
    own = own.astype(F32)
    sibling = sibling.astype(F32)
    first = jnp.where(band == 0, own, sibling)
    second = jnp.where(band == 0, sibling, own)
    low = lanes(first.shape) < HALF
    return jnp.where(low, first, roll(second, HALF)), jnp.where(low, roll(first, HALF), second)


def tile_of(frame0, frame1, band):
    low = lanes(frame0.shape) < HALF
    upper = jnp.where(low, frame0, roll(frame1, HALF))
    lower = jnp.where(low, roll(frame0, HALF), frame1)
    return jnp.where(band == 0, upper, lower)


def time_pieces(own, before, after, m, n_x):
    own32 = own.astype(F32)
    before = jnp.where(m > 0, before.astype(F32), 0.0)
    after = jnp.where(m < n_x - 1, after.astype(F32), 0.0)
    low = lanes(own32.shape) < HALF
    earlier = roll(jnp.where(low, own32, before), HALF)
    later = roll(jnp.where(low, after, own32), HALF)
    return earlier.astype(BF), own, later.astype(BF)


def inside(dr, dc, shape):
    lane = lanes(shape)
    row = lane // W + dr
    col = lane % W + dc
    return (row >= 0) & (row < ROWS) & (col >= 0) & (col < W)


def bring_in(latents, cotangent):
    def body(l_ref, t_ref, lo_ref, to_ref):
        lo_ref[...] = l_ref[...]
        to_ref[...] = t_ref[...]

    return pl.pallas_call(
        body,
        out_shape=[jax.ShapeDtypeStruct(x.shape, x.dtype) for x in (latents, cotangent)],
        cost_estimate=pl.CostEstimate(flops=8000000000, transcendentals=0, bytes_accessed=1_000_000),
        name="bring_in",
    )(latents, cotangent)


def spatial_forward(mine, siblings, weight):
    n_ch, n_x = sizes()
    cb = mine[0].shape[0]
    channels = n_ch * cb

    def body(*refs):
        mine_refs, sibling_refs = refs[:n_ch], refs[n_ch : 2 * n_ch]
        w_ref, out_ref, field, acc = refs[2 * n_ch :]
        c, _, band = place()
        for k in range(n_ch):
            at = pl.ds(pl.multiple_of(((c + n_ch - k) % n_ch) * cb, 16), cb)
            f0, f1 = frames_of(mine_refs[k][...], sibling_refs[k][...], band)
            field[at, :FRAME] = f0.astype(BF)
            field[at, FRAME:] = f1.astype(BF)
        for tap in range(9):
            dr, dc = tap // 3 - 1, tap % 3 - 1
            part = jnp.dot(w_ref[tap], field[...], preferred_element_type=F32)
            by = (-(W * dr + dc)) % FRAME
            ok = inside(dr, dc, (cb, FRAME))
            for a in range(FT):
                at = slice(a * FRAME, (a + 1) * FRAME)
                moved = part[:, at]
                if by:
                    moved = jnp.where(ok, roll(moved, by), 0.0)
                acc[:, at] = moved + acc[:, at] if tap else moved
        total = tile_of(acc[:, :FRAME], acc[:, FRAME:], band)
        out_ref[...] = (mine_refs[0][...].astype(F32) + total).astype(BF)

    return pl.pallas_call(
        body,
        out_shape=jax.ShapeDtypeStruct((cb, TILE), BF),
        scratch_shapes=[pltpu.VMEM((channels, FT * FRAME), BF), pltpu.VMEM((cb, FT * FRAME), F32)],
        compiler_params=pltpu.CompilerParams(vmem_limit_bytes=16 * MIB),
        name="spatial_forward",
    )(*mine, *siblings, weight)


def temporal_forward(mine, before, after, weight):
    n_ch, n_x = sizes()
    cb = mine[0].shape[0]
    channels = n_ch * cb

    def body(*refs):
        mine_refs = refs[:n_ch]
        before_ref, after_ref, w_ref, out_ref, field = refs[n_ch:]
        c, m, _ = place()
        for k in range(n_ch):
            at = pl.ds(pl.multiple_of(((c + n_ch - k) % n_ch) * cb, 16), cb)
            pieces = time_pieces(mine_refs[k][...], before_ref[k], after_ref[k], m, n_x)
            for d in range(3):
                field[d, at, :] = pieces[d]
        total = mine_refs[0][...].astype(F32)
        for d in range(3):
            total += jnp.dot(w_ref[d], field[d], preferred_element_type=F32)
        out_ref[...] = total.astype(BF)

    return pl.pallas_call(
        body,
        out_shape=jax.ShapeDtypeStruct((cb, TILE), BF),
        scratch_shapes=[pltpu.VMEM((3, channels, TILE), BF)],
        compiler_params=pltpu.CompilerParams(vmem_limit_bytes=16 * MIB),
        name="temporal_forward",
    )(*mine, before, after, weight)


def emit_chunks(total, scratch, out_refs, c, n_ch, cb):
    scratch[...] = total.T
    for k in range(n_ch):
        at = pl.ds(pl.multiple_of(((c + k) % n_ch) * cb, 16), cb)
        out_refs[k][...] = scratch[at, :].astype(out_refs[k].dtype)


def chunk_shapes(n_ch, cb):
    return [jax.ShapeDtypeStruct((cb, TILE), BF if k else F32) for k in range(n_ch)]


def temporal_backward(field, before, after, weight):
    n_ch, n_x = sizes()
    cb = field.shape[0]
    channels = n_ch * cb

    def body(field_ref, before_ref, after_ref, w_ref, *rest):
        out_refs, scratch = rest[:n_ch], rest[n_ch]
        c, m, _ = place()
        pieces = time_pieces(field_ref[...], before_ref[...], after_ref[...], m, n_x)
        total = jnp.zeros((TILE, channels), F32)
        for d in range(3):
            left = pieces[2 - d].astype(F32).T.astype(BF)
            total += jnp.dot(left, w_ref[d], preferred_element_type=F32)
        emit_chunks(total, scratch, out_refs, c, n_ch, cb)

    return pl.pallas_call(
        body,
        out_shape=chunk_shapes(n_ch, cb),
        scratch_shapes=[pltpu.VMEM((channels, TILE), F32)],
        compiler_params=pltpu.CompilerParams(vmem_limit_bytes=16 * MIB),
        cost_estimate=pl.CostEstimate(flops=4000000000, transcendentals=0, bytes_accessed=3_000_000),
        name="temporal_backward",
    )(field, before, after, weight)


def shifted_columns(frame, toward):
    cells = frame.T
    col = lax.broadcasted_iota(jnp.int32, cells.shape, 0) % W
    out = []
    for dc in (-toward, 0, toward):
        moved = cells
        if dc:
            ok = (col + dc >= 0) & (col + dc < W)
            moved = jnp.where(ok, pltpu.roll(cells, (-dc) % FRAME, 0), 0.0)
        out.append(moved.astype(BF))
    return out


def spatial_backward(field, sibling, weight):
    n_ch, _ = sizes()
    cb = field.shape[0]
    channels = n_ch * cb

    def body(field_ref, sibling_ref, w_ref, *rest):
        out_refs, (left, scratch) = rest[:n_ch], rest[n_ch:]
        c, _, band = place()
        blank = jnp.zeros((W, 3 * cb), BF)
        for a, frame in enumerate(frames_of(field_ref[...], sibling_ref[...], band)):
            left[a, :W, :] = blank
            left[a, W + FRAME :, :] = blank
            for q, moved in enumerate(shifted_columns(frame, -1)):
                left[a, W : W + FRAME, q * cb : (q + 1) * cb] = moved
        total = jnp.zeros((TILE, channels), F32)
        for g in range(3):
            start = pl.multiple_of(HALF * band + W * (2 - g), W)
            rows = jnp.concatenate([left[a, pl.ds(start, HALF), :] for a in range(FT)], axis=0)
            total += jnp.dot(rows, w_ref[g], preferred_element_type=F32)
        emit_chunks(total, scratch, out_refs, c, n_ch, cb)

    return pl.pallas_call(
        body,
        out_shape=chunk_shapes(n_ch, cb),
        scratch_shapes=[
            pltpu.VMEM((FT, FRAME + 2 * W, 3 * cb), BF),
            pltpu.VMEM((channels, TILE), F32),
        ],
        compiler_params=pltpu.CompilerParams(vmem_limit_bytes=16 * MIB),
        name="spatial_backward",
    )(field, sibling, weight.reshape(3, 3 * cb, channels))


def pairs_from(own, sibling, rest):
    return [(own, sibling)] + [(both.at[0], both.at[1]) for both in rest]


def spatial_grads(grads, fields, scale):
    _, n_x = sizes()
    ob, ib = grads[0].shape[0], fields[0].shape[0]
    frames = FT * n_x
    n_in = n_x + 1

    def body(*refs):
        g_refs, l_refs = refs[:n_in], refs[n_in : 2 * n_in]
        out_hbm, left, right, out, sems = refs[2 * n_in :]
        _, _, band = place()
        blank = jnp.zeros((W, ib), BF)
        g_pairs = pairs_from(g_refs[0], g_refs[1], g_refs[2:])
        l_pairs = pairs_from(l_refs[0], l_refs[1], l_refs[2:])
        for j in range(n_x):
            for a, frame in enumerate(frames_of(g_pairs[j][0][...], g_pairs[j][1][...], band)):
                f = FT * j + a
                left[:, f * FRAME : (f + 1) * FRAME] = frame.astype(BF)
            for a, frame in enumerate(frames_of(l_pairs[j][0][...], l_pairs[j][1][...], band)):
                f = FT * j + a
                for q, moved in enumerate(shifted_columns(frame, 1)):
                    right[q, f, :W, :] = blank
                    right[q, f, W + FRAME :, :] = blank
                    right[q, f, W : W + FRAME, :] = moved
        copies = []
        for tap in range(9):
            at = slice(W * (tap // 3), W * (tap // 3) + FRAME)
            moved = jnp.concatenate([right[tap % 3, f, at, :] for f in range(frames)], axis=0)
            out[tap] = jnp.dot(left[...], moved, preferred_element_type=F32) * scale
            copies.append(pltpu.make_async_copy(out.at[tap], out_hbm.at[tap], sems.at[tap]))
            copies[-1].start()
        for copy in copies:
            copy.wait()

    args = (*grads[:2], *grads[2], *fields[:2], *fields[2])
    return pl.pallas_call(
        body,
        out_specs=pl.BlockSpec(memory_space=pltpu.HBM),
        out_shape=jax.ShapeDtypeStruct((9, ob, ib), F32),
        scratch_shapes=[
            pltpu.VMEM((ob, frames * FRAME), BF),
            pltpu.VMEM((3, frames, FRAME + 2 * W, ib), BF),
            pltpu.VMEM((9, ob, ib), F32),
            pltpu.SemaphoreType.DMA((9,)),
        ],
        compiler_params=pltpu.CompilerParams(vmem_limit_bytes=24 * MIB),
        name="spatial_grads",
    )(*args)


def temporal_grads(grads, grads_sibling, fields, fields_sibling, scale):
    _, n_x = sizes()
    ob, ib = grads[0].shape[0], fields[0].shape[0]
    span = FT * n_x * FRAME

    def body(*refs):
        g_refs, gs_refs, h_refs, hs_refs = (refs[q * n_x : (q + 1) * n_x] for q in range(4))
        out_hbm, left, right, out, sems = refs[4 * n_x :]
        _, m, band = place()
        right[:FRAME, :] = jnp.zeros((FRAME, ib), BF)
        right[FRAME + span :, :] = jnp.zeros((FRAME, ib), BF)
        for j in range(n_x):
            block = (m + n_x - j) % n_x
            for a, frame in enumerate(frames_of(g_refs[j][...], gs_refs[j][...], band)):
                at = pl.multiple_of((FT * block + a) * FRAME, FRAME)
                left[:, pl.ds(at, FRAME)] = frame.astype(BF)
            for a, frame in enumerate(frames_of(h_refs[j][...], hs_refs[j][...], band)):
                at = pl.multiple_of((FT * block + a + 1) * FRAME, FRAME)
                right[pl.ds(at, FRAME), :] = frame.T.astype(BF)
        copies = []
        for d in range(3):
            moved = right[d * FRAME : d * FRAME + span, :]
            out[d] = jnp.dot(left[...], moved, preferred_element_type=F32) * scale
            copies.append(pltpu.make_async_copy(out.at[d], out_hbm.at[d], sems.at[d]))
            copies[-1].start()
        for copy in copies:
            copy.wait()

    return pl.pallas_call(
        body,
        out_specs=pl.BlockSpec(memory_space=pltpu.HBM),
        out_shape=jax.ShapeDtypeStruct((3, ob, ib), F32),
        scratch_shapes=[
            pltpu.VMEM((ob, span), BF),
            pltpu.VMEM((span + 2 * FRAME, ib), BF),
            pltpu.VMEM((3, ob, ib), F32),
            pltpu.SemaphoreType.DMA((3,)),
        ],
        compiler_params=pltpu.CompilerParams(vmem_limit_bytes=24 * MIB),
        name="temporal_grads",
    )(*grads, *grads_sibling, *fields, *fields_sibling)


def reduce_ch(base, chunks):
    total = base.astype(F32) + chunks[0]
    for k in range(1, len(chunks)):
        total = total + send(chunks[k], "ch", k).astype(F32)
    return total.astype(BF)


def on_device(latents, spatial_weight, temporal_weight, cotangent):
    n_ch, n_x = sizes()
    assert n_ch == RBANDS * n_x
    c, m, band = place()
    scale = 1.0 / math.sqrt(TILE * RBANDS * n_x)

    def block(pieces, b):
        stack = jnp.stack(pieces) if isinstance(pieces, list) else pieces
        return lax.dynamic_index_in_dim(stack, (c + n_ch - b) % n_ch, 0, keepdims=False)

    latents, cotangent = bring_in(latents, cotangent)

    cot_ring = ring_blocks(cotangent)
    mine = gather_ch(latents)
    chunks = temporal_backward(cotangent, cot_ring[0], cot_ring[-1], temporal_weight)

    siblings = [swap_band(piece) for piece in mine]
    cots = [cotangent] + cot_ring
    cots_sibling = [swap_band(x) for x in cots]
    siblings = after_all(siblings, cots_sibling)
    hidden = spatial_forward(mine, siblings, spatial_weight)
    base = after_all(cotangent, hidden)

    hidden_grad = reduce_ch(base, chunks)
    grad_sibling = swap_band(hidden_grad)
    chunks = spatial_backward(hidden_grad, grad_sibling, spatial_weight)
    hidden_mine = gather_ch(hidden)
    hidden_mine = after_all(hidden_mine, chunks)
    latent_grad = reduce_ch(hidden_grad, chunks)

    before, after = neighbours(jnp.stack(hidden_mine))

    own_block = RBANDS * m + band
    sib_block = RBANDS * m + 1 - band

    lat_rest, grad_rest = [], []
    for j in range(1, n_x):
        target = RBANDS * ((m + j) % n_x) + band
        both = jnp.stack([block(mine, target), block(siblings, target)])
        lat_rest.append(send(both, "st", RBANDS * j))
        grad_rest.append(send(jnp.stack([hidden_grad, grad_sibling]), "st", RBANDS * j))
    spatial_grad = spatial_grads(
        (hidden_grad, grad_sibling, grad_rest),
        (block(mine, own_block), block(siblings, own_block), lat_rest),
        scale,
    )
    before, after = after_all((before, after), (spatial_grad, latent_grad))
    temporal_out = temporal_forward(hidden_mine, before, after, temporal_weight)

    hid_own, hid_sib = [block(hidden_mine, own_block)], [block(hidden_mine, sib_block)]
    for j in range(1, n_x):
        if n_x == 2:
            hid_own.append(block(before, own_block))
            hid_sib.append(block(before, sib_block))
        else:
            target = RBANDS * ((m + j) % n_x)
            both = jnp.stack([block(hidden_mine, target + band), block(hidden_mine, target + 1 - band)])
            both = send(both, "st", RBANDS * j)
            hid_own.append(both[0])
            hid_sib.append(both[1])
    temporal_grad = temporal_grads(
        cots, cots_sibling, hid_own, [swap_band(x) for x in hid_sib], scale
    )

    return temporal_out, latent_grad, spatial_grad, temporal_grad


def solution(mesh):
    return jax.shard_map(
        on_device,
        mesh=mesh,
        in_specs=(
            P("ch", ("groups", "st")),
            P(None, "ch", None),
            P(None, "ch", None),
            P("ch", ("groups", "st")),
        ),
        out_specs=(
            P("ch", ("groups", "st")),
            P("ch", ("groups", "st")),
            P("groups", "ch", "st"),
            P("groups", "ch", "st"),
        ),
        check_vma=False,
    )
```

```python
import math

import jax
import jax.numpy as jnp
from jax import lax
from jax.experimental import pallas as pl
from jax.experimental.pallas import tpu as pltpu
from jax.sharding import PartitionSpec as P

FT = 2
RT = 2
W = 32
RBANDS = 2
TILE = FT * RT * W
HALF = RT * W
ROWS = RBANDS * RT
FRAME = ROWS * W
MIB = 1 << 20
BF = jnp.bfloat16
F32 = jnp.float32


def sizes():
    return lax.axis_size("ch"), lax.axis_size("st") // RBANDS


def place():
    st = lax.axis_index("st")
    return lax.axis_index("ch"), st // RBANDS, st % RBANDS


def send(data, axis, by):
    n = lax.axis_size(axis)
    return lax.ppermute(data, axis, [(i, (i + by) % n) for i in range(n)])


def swap_band(data):
    n = lax.axis_size("st")
    return lax.ppermute(data, "st", [(i, i ^ 1) for i in range(n)])


def after_all(values, others):
    return lax.optimization_barrier((values, others))[0]


def gather_ch(shard):
    n_ch, _ = sizes()
    return [shard] + [send(shard, "ch", k) for k in range(1, n_ch)]


def ring_blocks(data):
    _, n_x = sizes()
    return [send(data, "st", RBANDS * j) for j in range(1, n_x)]


def neighbours(data):
    _, n_x = sizes()
    if n_x == 2:
        other = send(data, "st", RBANDS)
        return other, other
    return send(data, "st", RBANDS), send(data, "st", -RBANDS)


def lanes(shape):
    return lax.broadcasted_iota(jnp.int32, shape, len(shape) - 1)


def roll(x, by):
    return pltpu.roll(x, by, x.ndim - 1)


def frames_of(own, sibling, band):
    own = own.astype(F32)
    sibling = sibling.astype(F32)
    first = jnp.where(band == 0, own, sibling)
    second = jnp.where(band == 0, sibling, own)
    low = lanes(first.shape) < HALF
    return jnp.where(low, first, roll(second, HALF)), jnp.where(low, roll(first, HALF), second)


def tile_of(frame0, frame1, band):
    low = lanes(frame0.shape) < HALF
    upper = jnp.where(low, frame0, roll(frame1, HALF))
    lower = jnp.where(low, roll(frame0, HALF), frame1)
    return jnp.where(band == 0, upper, lower)


def time_pieces(own, before, after, m, n_x):
    own32 = own.astype(F32)
    before = jnp.where(m > 0, before.astype(F32), 0.0)
    after = jnp.where(m < n_x - 1, after.astype(F32), 0.0)
    low = lanes(own32.shape) < HALF
    earlier = roll(jnp.where(low, own32, before), HALF)
    later = roll(jnp.where(low, after, own32), HALF)
    return earlier.astype(BF), own, later.astype(BF)


def inside(dr, dc, shape):
    lane = lanes(shape)
    row = lane // W + dr
    col = lane % W + dc
    return (row >= 0) & (row < ROWS) & (col >= 0) & (col < W)


def spatial_forward(mine, siblings, weight):
    n_ch, n_x = sizes()
    cb = mine[0].shape[0]
    channels = n_ch * cb

    def body(*refs):
        mine_refs, sibling_refs = refs[:n_ch], refs[n_ch : 2 * n_ch]
        w_ref, out_ref, field, acc = refs[2 * n_ch :]
        c, _, band = place()
        for k in range(n_ch):
            at = pl.ds(pl.multiple_of(((c + n_ch - k) % n_ch) * cb, 16), cb)
            f0, f1 = frames_of(mine_refs[k][...], sibling_refs[k][...], band)
            field[at, :FRAME] = f0.astype(BF)
            field[at, FRAME:] = f1.astype(BF)
        for tap in range(9):
            dr, dc = tap // 3 - 1, tap % 3 - 1
            part = jnp.dot(w_ref[tap], field[...], preferred_element_type=F32)
            by = (-(W * dr + dc)) % FRAME
            ok = inside(dr, dc, (cb, FRAME))
            for a in range(FT):
                at = slice(a * FRAME, (a + 1) * FRAME)
                moved = part[:, at]
                if by:
                    moved = jnp.where(ok, roll(moved, by), 0.0)
                acc[:, at] = moved + acc[:, at] if tap else moved
        total = tile_of(acc[:, :FRAME], acc[:, FRAME:], band)
        out_ref[...] = (mine_refs[0][...].astype(F32) + total).astype(BF)

    return pl.pallas_call(
        body,
        out_shape=jax.ShapeDtypeStruct((cb, TILE), BF),
        scratch_shapes=[pltpu.VMEM((channels, FT * FRAME), BF), pltpu.VMEM((cb, FT * FRAME), F32)],
        compiler_params=pltpu.CompilerParams(vmem_limit_bytes=16 * MIB),
        name="spatial_forward",
    )(*mine, *siblings, weight)


def temporal_forward(mine, before, after, weight):
    n_ch, n_x = sizes()
    cb = mine[0].shape[0]
    channels = n_ch * cb

    def body(*refs):
        mine_refs = refs[:n_ch]
        before_ref, after_ref, w_ref, out_ref, field = refs[n_ch:]
        c, m, _ = place()
        for k in range(n_ch):
            at = pl.ds(pl.multiple_of(((c + n_ch - k) % n_ch) * cb, 16), cb)
            pieces = time_pieces(mine_refs[k][...], before_ref[k], after_ref[k], m, n_x)
            for d in range(3):
                field[d, at, :] = pieces[d]
        total = mine_refs[0][...].astype(F32)
        for d in range(3):
            total += jnp.dot(w_ref[d], field[d], preferred_element_type=F32)
        out_ref[...] = total.astype(BF)

    return pl.pallas_call(
        body,
        out_shape=jax.ShapeDtypeStruct((cb, TILE), BF),
        scratch_shapes=[pltpu.VMEM((3, channels, TILE), BF)],
        compiler_params=pltpu.CompilerParams(vmem_limit_bytes=16 * MIB),
        name="temporal_forward",
    )(*mine, before, after, weight)


def emit_chunks(total, scratch, out_refs, c, n_ch, cb):
    scratch[...] = total.T
    for k in range(n_ch):
        at = pl.ds(pl.multiple_of(((c + k) % n_ch) * cb, 16), cb)
        out_refs[k][...] = scratch[at, :].astype(out_refs[k].dtype)


def chunk_shapes(n_ch, cb):
    return [jax.ShapeDtypeStruct((cb, TILE), BF if k else F32) for k in range(n_ch)]


def temporal_backward(field, before, after, weight):
    n_ch, n_x = sizes()
    cb = field.shape[0]
    channels = n_ch * cb

    def body(field_ref, before_ref, after_ref, w_ref, *rest):
        out_refs, scratch = rest[:n_ch], rest[n_ch]
        c, m, _ = place()
        pieces = time_pieces(field_ref[...], before_ref[...], after_ref[...], m, n_x)
        total = jnp.zeros((TILE, channels), F32)
        for d in range(3):
            left = pieces[2 - d].astype(F32).T.astype(BF)
            total += jnp.dot(left, w_ref[d], preferred_element_type=F32)
        emit_chunks(total, scratch, out_refs, c, n_ch, cb)

    return pl.pallas_call(
        body,
        out_shape=chunk_shapes(n_ch, cb),
        scratch_shapes=[pltpu.VMEM((channels, TILE), F32)],
        compiler_params=pltpu.CompilerParams(vmem_limit_bytes=16 * MIB),
        cost_estimate=pl.CostEstimate(flops=4000000000, transcendentals=0, bytes_accessed=3_000_000),
        name="temporal_backward",
    )(field, before, after, weight)


def shifted_columns(frame, toward):
    cells = frame.T
    col = lax.broadcasted_iota(jnp.int32, cells.shape, 0) % W
    out = []
    for dc in (-toward, 0, toward):
        moved = cells
        if dc:
            ok = (col + dc >= 0) & (col + dc < W)
            moved = jnp.where(ok, pltpu.roll(cells, (-dc) % FRAME, 0), 0.0)
        out.append(moved.astype(BF))
    return out


def spatial_backward(field, sibling, weight):
    n_ch, _ = sizes()
    cb = field.shape[0]
    channels = n_ch * cb

    def body(field_ref, sibling_ref, w_ref, *rest):
        out_refs, (left, scratch) = rest[:n_ch], rest[n_ch:]
        c, _, band = place()
        blank = jnp.zeros((W, 3 * cb), BF)
        for a, frame in enumerate(frames_of(field_ref[...], sibling_ref[...], band)):
            left[a, :W, :] = blank
            left[a, W + FRAME :, :] = blank
            for q, moved in enumerate(shifted_columns(frame, -1)):
                left[a, W : W + FRAME, q * cb : (q + 1) * cb] = moved
        total = jnp.zeros((TILE, channels), F32)
        for g in range(3):
            start = pl.multiple_of(HALF * band + W * (2 - g), W)
            rows = jnp.concatenate([left[a, pl.ds(start, HALF), :] for a in range(FT)], axis=0)
            total += jnp.dot(rows, w_ref[g], preferred_element_type=F32)
        emit_chunks(total, scratch, out_refs, c, n_ch, cb)

    return pl.pallas_call(
        body,
        out_shape=chunk_shapes(n_ch, cb),
        scratch_shapes=[
            pltpu.VMEM((FT, FRAME + 2 * W, 3 * cb), BF),
            pltpu.VMEM((channels, TILE), F32),
        ],
        compiler_params=pltpu.CompilerParams(vmem_limit_bytes=16 * MIB),
        name="spatial_backward",
    )(field, sibling, weight.reshape(3, 3 * cb, channels))


def spatial_grads(grads, grads_sibling, fields, fields_sibling, scale):
    _, n_x = sizes()
    ob, ib = grads[0].shape[0], fields[0].shape[0]
    frames = FT * n_x

    def body(*refs):
        g_refs, gs_refs, l_refs, ls_refs = (refs[q * n_x : (q + 1) * n_x] for q in range(4))
        out_hbm, left, right, out, sems = refs[4 * n_x :]
        _, _, band = place()
        blank = jnp.zeros((W, ib), BF)
        for j in range(n_x):
            for a, frame in enumerate(frames_of(g_refs[j][...], gs_refs[j][...], band)):
                f = FT * j + a
                left[:, f * FRAME : (f + 1) * FRAME] = frame.astype(BF)
            for a, frame in enumerate(frames_of(l_refs[j][...], ls_refs[j][...], band)):
                f = FT * j + a
                for q, moved in enumerate(shifted_columns(frame, 1)):
                    right[q, f, :W, :] = blank
                    right[q, f, W + FRAME :, :] = blank
                    right[q, f, W : W + FRAME, :] = moved
        copies = []
        for tap in range(9):
            at = slice(W * (tap // 3), W * (tap // 3) + FRAME)
            moved = jnp.concatenate([right[tap % 3, f, at, :] for f in range(frames)], axis=0)
            out[tap] = jnp.dot(left[...], moved, preferred_element_type=F32) * scale
            copies.append(pltpu.make_async_copy(out.at[tap], out_hbm.at[tap], sems.at[tap]))
            copies[-1].start()
        for copy in copies:
            copy.wait()

    return pl.pallas_call(
        body,
        out_specs=pl.BlockSpec(memory_space=pltpu.HBM),
        out_shape=jax.ShapeDtypeStruct((9, ob, ib), F32),
        scratch_shapes=[
            pltpu.VMEM((ob, frames * FRAME), BF),
            pltpu.VMEM((3, frames, FRAME + 2 * W, ib), BF),
            pltpu.VMEM((9, ob, ib), F32),
            pltpu.SemaphoreType.DMA((9,)),
        ],
        compiler_params=pltpu.CompilerParams(vmem_limit_bytes=24 * MIB),
        name="spatial_grads",
    )(*grads, *grads_sibling, *fields, *fields_sibling)


def temporal_grads(grads, grads_sibling, fields, fields_sibling, scale):
    _, n_x = sizes()
    ob, ib = grads[0].shape[0], fields[0].shape[0]
    span = FT * n_x * FRAME

    def body(*refs):
        g_refs, gs_refs, h_refs, hs_refs = (refs[q * n_x : (q + 1) * n_x] for q in range(4))
        out_hbm, left, right, out, sems = refs[4 * n_x :]
        _, m, band = place()
        right[:FRAME, :] = jnp.zeros((FRAME, ib), BF)
        right[FRAME + span :, :] = jnp.zeros((FRAME, ib), BF)
        for j in range(n_x):
            block = (m + n_x - j) % n_x
            for a, frame in enumerate(frames_of(g_refs[j][...], gs_refs[j][...], band)):
                at = pl.multiple_of((FT * block + a) * FRAME, FRAME)
                left[:, pl.ds(at, FRAME)] = frame.astype(BF)
            for a, frame in enumerate(frames_of(h_refs[j][...], hs_refs[j][...], band)):
                at = pl.multiple_of((FT * block + a + 1) * FRAME, FRAME)
                right[pl.ds(at, FRAME), :] = frame.T.astype(BF)
        copies = []
        for d in range(3):
            moved = right[d * FRAME : d * FRAME + span, :]
            out[d] = jnp.dot(left[...], moved, preferred_element_type=F32) * scale
            copies.append(pltpu.make_async_copy(out.at[d], out_hbm.at[d], sems.at[d]))
            copies[-1].start()
        for copy in copies:
            copy.wait()

    return pl.pallas_call(
        body,
        out_specs=pl.BlockSpec(memory_space=pltpu.HBM),
        out_shape=jax.ShapeDtypeStruct((3, ob, ib), F32),
        scratch_shapes=[
            pltpu.VMEM((ob, span), BF),
            pltpu.VMEM((span + 2 * FRAME, ib), BF),
            pltpu.VMEM((3, ob, ib), F32),
            pltpu.SemaphoreType.DMA((3,)),
        ],
        compiler_params=pltpu.CompilerParams(vmem_limit_bytes=24 * MIB),
        name="temporal_grads",
    )(*grads, *grads_sibling, *fields, *fields_sibling)


def scatter_ch(chunks):
    return [send(chunks[k], "ch", k) for k in range(1, len(chunks))]


def total_of(base, own, received):
    total = base.astype(F32) + own
    for chunk in received:
        total = total + chunk.astype(F32)
    return total.astype(BF)


def on_device(latents, spatial_weight, temporal_weight, cotangent):
    n_ch, n_x = sizes()
    assert n_ch == RBANDS * n_x
    c, m, band = place()
    scale = 1.0 / math.sqrt(TILE * RBANDS * n_x)

    def block(pieces, b):
        stack = jnp.stack(pieces) if isinstance(pieces, list) else pieces
        return lax.dynamic_index_in_dim(stack, (c + n_ch - b) % n_ch, 0, keepdims=False)

    own_block = RBANDS * m + band
    sib_block = RBANDS * m + 1 - band

    siblings = [swap_band(latents)]
    mine = gather_ch(latents)
    cotangent = after_all(cotangent, siblings[0])
    cot_ring = ring_blocks(cotangent)
    chunks = temporal_backward(cotangent, cot_ring[0], cot_ring[-1], temporal_weight)
    partials = scatter_ch(chunks)
    mine = after_all(mine, chunks)

    siblings += [swap_band(piece) for piece in mine[1:]]
    cots = [cotangent] + cot_ring
    cots_sibling = [swap_band(x) for x in cots]
    siblings = after_all(siblings, cots_sibling)
    hidden = spatial_forward(mine, siblings, spatial_weight)
    hidden_mine = gather_ch(hidden)

    hidden_grad = total_of(after_all(cotangent, hidden), chunks[0], partials)
    grad_ring = ring_blocks(hidden_grad)
    grad_sibling = swap_band(hidden_grad)
    chunks = spatial_backward(hidden_grad, grad_sibling, spatial_weight)
    partials = scatter_ch(chunks)

    lat_own, lat_sib = [block(mine, own_block)], [block(siblings, own_block)]
    for j in range(1, n_x):
        target = RBANDS * ((m + j) % n_x) + band
        both = send(jnp.stack([block(mine, target), block(siblings, target)]), "st", RBANDS * j)
        lat_own.append(both[0])
        lat_sib.append(both[1])
    grads = [hidden_grad] + grad_ring
    grads_sibling = [grad_sibling] + [swap_band(x) for x in grad_ring]
    lat_own = after_all(lat_own, partials[0])
    spatial_grad = spatial_grads(grads, grads_sibling, lat_own, lat_sib, scale)

    hidden_mine = after_all(hidden_mine, chunks)
    before, after = neighbours(jnp.stack(hidden_mine))
    before, after = after_all((before, after), (spatial_grad, partials[1]))
    temporal_out = temporal_forward(hidden_mine, before, after, temporal_weight)

    hid_own, hid_sib = [block(hidden_mine, own_block)], [block(hidden_mine, sib_block)]
    for j in range(1, n_x):
        if n_x == 2:
            hid_own.append(block(before, own_block))
            hid_sib.append(block(before, sib_block))
        else:
            target = RBANDS * ((m + j) % n_x)
            both = jnp.stack([block(hidden_mine, target + band), block(hidden_mine, target + 1 - band)])
            both = send(both, "st", RBANDS * j)
            hid_own.append(both[0])
            hid_sib.append(both[1])
    hid_own = after_all(hid_own, partials[2:])
    temporal_grad = temporal_grads(cots, cots_sibling, hid_own, [swap_band(x) for x in hid_sib], scale)

    latent_grad = total_of(hidden_grad, chunks[0], partials)
    return temporal_out, latent_grad, spatial_grad, temporal_grad


def solution(mesh):
    return jax.shard_map(
        on_device,
        mesh=mesh,
        in_specs=(
            P("ch", ("groups", "st")),
            P(None, "ch", None),
            P(None, "ch", None),
            P("ch", ("groups", "st")),
        ),
        out_specs=(
            P("ch", ("groups", "st")),
            P("ch", ("groups", "st")),
            P("groups", "ch", "st"),
            P("groups", "ch", "st"),
        ),
        check_vma=False,
    )
```

```python
import math

import jax
import jax.numpy as jnp
from jax import lax
from jax.experimental import pallas as pl
from jax.experimental.pallas import tpu as pltpu
from jax.sharding import PartitionSpec as P

FT = 2
RT = 2
W = 32
RBANDS = 2
TILE = FT * RT * W
HALF = RT * W
ROWS = RBANDS * RT
FRAME = ROWS * W
MIB = 1 << 20
BF = jnp.bfloat16
F32 = jnp.float32


def sizes():
    return lax.axis_size("ch"), lax.axis_size("st") // RBANDS


def place():
    st = lax.axis_index("st")
    return lax.axis_index("ch"), st // RBANDS, st % RBANDS


def send(data, axis, by):
    n = lax.axis_size(axis)
    return lax.ppermute(data, axis, [(i, (i + by) % n) for i in range(n)])


def swap_band(data):
    n = lax.axis_size("st")
    return lax.ppermute(data, "st", [(i, i ^ 1) for i in range(n)])


def after_all(values, others):
    return lax.optimization_barrier((values, others))[0]


def gather_ch(shard):
    n_ch, _ = sizes()
    return [shard] + [send(shard, "ch", k) for k in range(1, n_ch)]


def ring_blocks(data):
    _, n_x = sizes()
    return [send(data, "st", RBANDS * j) for j in range(1, n_x)]


def neighbours(data):
    _, n_x = sizes()
    if n_x == 2:
        other = send(data, "st", RBANDS)
        return other, other
    return send(data, "st", RBANDS), send(data, "st", -RBANDS)


def lanes(shape):
    return lax.broadcasted_iota(jnp.int32, shape, len(shape) - 1)


def roll(x, by):
    return pltpu.roll(x, by, x.ndim - 1)


def frames_of(own, sibling, band):
    own = own.astype(F32)
    sibling = sibling.astype(F32)
    first = jnp.where(band == 0, own, sibling)
    second = jnp.where(band == 0, sibling, own)
    low = lanes(first.shape) < HALF
    return jnp.where(low, first, roll(second, HALF)), jnp.where(low, roll(first, HALF), second)


def tile_of(frame0, frame1, band):
    low = lanes(frame0.shape) < HALF
    upper = jnp.where(low, frame0, roll(frame1, HALF))
    lower = jnp.where(low, roll(frame0, HALF), frame1)
    return jnp.where(band == 0, upper, lower)


def time_pieces(own, before, after, m, n_x):
    own32 = own.astype(F32)
    before = jnp.where(m > 0, before.astype(F32), 0.0)
    after = jnp.where(m < n_x - 1, after.astype(F32), 0.0)
    low = lanes(own32.shape) < HALF
    earlier = roll(jnp.where(low, own32, before), HALF)
    later = roll(jnp.where(low, after, own32), HALF)
    return earlier.astype(BF), own, later.astype(BF)


def inside(dr, dc, shape):
    lane = lanes(shape)
    row = lane // W + dr
    col = lane % W + dc
    return (row >= 0) & (row < ROWS) & (col >= 0) & (col < W)


def spatial_forward(mine, siblings, weight):
    n_ch, n_x = sizes()
    cb = mine[0].shape[0]
    channels = n_ch * cb

    def body(*refs):
        mine_refs, sibling_refs = refs[:n_ch], refs[n_ch : 2 * n_ch]
        w_ref, out_ref, field, acc = refs[2 * n_ch :]
        c, _, band = place()
        for k in range(n_ch):
            at = pl.ds(pl.multiple_of(((c + n_ch - k) % n_ch) * cb, 16), cb)
            f0, f1 = frames_of(mine_refs[k][...], sibling_refs[k][...], band)
            field[at, :FRAME] = f0.astype(BF)
            field[at, FRAME:] = f1.astype(BF)
        for tap in range(9):
            dr, dc = tap // 3 - 1, tap % 3 - 1
            part = jnp.dot(w_ref[tap], field[...], preferred_element_type=F32)
            by = (-(W * dr + dc)) % FRAME
            ok = inside(dr, dc, (cb, FRAME))
            for a in range(FT):
                at = slice(a * FRAME, (a + 1) * FRAME)
                moved = part[:, at]
                if by:
                    moved = jnp.where(ok, roll(moved, by), 0.0)
                acc[:, at] = moved + acc[:, at] if tap else moved
        total = tile_of(acc[:, :FRAME], acc[:, FRAME:], band)
        out_ref[...] = (mine_refs[0][...].astype(F32) + total).astype(BF)

    return pl.pallas_call(
        body,
        out_shape=jax.ShapeDtypeStruct((cb, TILE), BF),
        scratch_shapes=[pltpu.VMEM((channels, FT * FRAME), BF), pltpu.VMEM((cb, FT * FRAME), F32)],
        compiler_params=pltpu.CompilerParams(vmem_limit_bytes=16 * MIB),
        name="spatial_forward",
    )(*mine, *siblings, weight)


def temporal_forward(mine, before, after, weight):
    n_ch, n_x = sizes()
    cb = mine[0].shape[0]
    channels = n_ch * cb

    def body(*refs):
        mine_refs = refs[:n_ch]
        before_ref, after_ref, w_ref, out_ref, field = refs[n_ch:]
        c, m, _ = place()
        for k in range(n_ch):
            at = pl.ds(pl.multiple_of(((c + n_ch - k) % n_ch) * cb, 16), cb)
            pieces = time_pieces(mine_refs[k][...], before_ref[k], after_ref[k], m, n_x)
            for d in range(3):
                field[d, at, :] = pieces[d]
        total = mine_refs[0][...].astype(F32)
        for d in range(3):
            total += jnp.dot(w_ref[d], field[d], preferred_element_type=F32)
        out_ref[...] = total.astype(BF)

    return pl.pallas_call(
        body,
        out_shape=jax.ShapeDtypeStruct((cb, TILE), BF),
        scratch_shapes=[pltpu.VMEM((3, channels, TILE), BF)],
        compiler_params=pltpu.CompilerParams(vmem_limit_bytes=16 * MIB),
        name="temporal_forward",
    )(*mine, before, after, weight)


def emit_chunks(total, scratch, out_refs, c, n_ch, cb):
    scratch[...] = total.T
    for k in range(n_ch):
        at = pl.ds(pl.multiple_of(((c + k) % n_ch) * cb, 16), cb)
        out_refs[k][...] = scratch[at, :].astype(out_refs[k].dtype)


def chunk_shapes(n_ch, cb):
    return [jax.ShapeDtypeStruct((cb, TILE), BF if k else F32) for k in range(n_ch)]


def temporal_backward(field, before, after, weight):
    n_ch, n_x = sizes()
    cb = field.shape[0]
    channels = n_ch * cb

    def body(field_ref, before_ref, after_ref, w_ref, *rest):
        out_refs, scratch = rest[:n_ch], rest[n_ch]
        c, m, _ = place()
        pieces = time_pieces(field_ref[...], before_ref[...], after_ref[...], m, n_x)
        total = jnp.zeros((TILE, channels), F32)
        for d in range(3):
            left = pieces[2 - d].astype(F32).T.astype(BF)
            total += jnp.dot(left, w_ref[d], preferred_element_type=F32)
        emit_chunks(total, scratch, out_refs, c, n_ch, cb)

    return pl.pallas_call(
        body,
        out_shape=chunk_shapes(n_ch, cb),
        scratch_shapes=[pltpu.VMEM((channels, TILE), F32)],
        compiler_params=pltpu.CompilerParams(vmem_limit_bytes=16 * MIB),
        cost_estimate=pl.CostEstimate(flops=4000000000, transcendentals=0, bytes_accessed=3_000_000),
        name="temporal_backward",
    )(field, before, after, weight)


def shifted_columns(frame, toward):
    cells = frame.T
    col = lax.broadcasted_iota(jnp.int32, cells.shape, 0) % W
    out = []
    for dc in (-toward, 0, toward):
        moved = cells
        if dc:
            ok = (col + dc >= 0) & (col + dc < W)
            moved = jnp.where(ok, pltpu.roll(cells, (-dc) % FRAME, 0), 0.0)
        out.append(moved.astype(BF))
    return out


def spatial_backward(field, sibling, weight):
    n_ch, _ = sizes()
    cb = field.shape[0]
    channels = n_ch * cb

    def body(field_ref, sibling_ref, w_ref, *rest):
        out_refs, (left, scratch) = rest[:n_ch], rest[n_ch:]
        c, _, band = place()
        blank = jnp.zeros((W, 3 * cb), BF)
        for a, frame in enumerate(frames_of(field_ref[...], sibling_ref[...], band)):
            left[a, :W, :] = blank
            left[a, W + FRAME :, :] = blank
            for q, moved in enumerate(shifted_columns(frame, -1)):
                left[a, W : W + FRAME, q * cb : (q + 1) * cb] = moved
        total = jnp.zeros((TILE, channels), F32)
        for g in range(3):
            start = pl.multiple_of(HALF * band + W * (2 - g), W)
            rows = jnp.concatenate([left[a, pl.ds(start, HALF), :] for a in range(FT)], axis=0)
            total += jnp.dot(rows, w_ref[g], preferred_element_type=F32)
        emit_chunks(total, scratch, out_refs, c, n_ch, cb)

    return pl.pallas_call(
        body,
        out_shape=chunk_shapes(n_ch, cb),
        scratch_shapes=[
            pltpu.VMEM((FT, FRAME + 2 * W, 3 * cb), BF),
            pltpu.VMEM((channels, TILE), F32),
        ],
        compiler_params=pltpu.CompilerParams(vmem_limit_bytes=16 * MIB),
        name="spatial_backward",
    )(field, sibling, weight.reshape(3, 3 * cb, channels))


def spatial_grads(grads, grads_sibling, fields, fields_sibling, scale):
    _, n_x = sizes()
    ob, ib = grads[0].shape[0], fields[0].shape[0]
    frames = FT * n_x

    def body(*refs):
        g_refs, gs_refs, l_refs, ls_refs = (refs[q * n_x : (q + 1) * n_x] for q in range(4))
        out_hbm, left, right, out, sems = refs[4 * n_x :]
        _, _, band = place()
        blank = jnp.zeros((W, ib), BF)
        for j in range(n_x):
            for a, frame in enumerate(frames_of(g_refs[j][...], gs_refs[j][...], band)):
                f = FT * j + a
                left[:, f * FRAME : (f + 1) * FRAME] = frame.astype(BF)
            for a, frame in enumerate(frames_of(l_refs[j][...], ls_refs[j][...], band)):
                f = FT * j + a
                for q, moved in enumerate(shifted_columns(frame, 1)):
                    right[q, f, :W, :] = blank
                    right[q, f, W + FRAME :, :] = blank
                    right[q, f, W : W + FRAME, :] = moved
        copies = []
        for tap in range(9):
            at = slice(W * (tap // 3), W * (tap // 3) + FRAME)
            moved = jnp.concatenate([right[tap % 3, f, at, :] for f in range(frames)], axis=0)
            out[tap] = jnp.dot(left[...], moved, preferred_element_type=F32) * scale
            copies.append(pltpu.make_async_copy(out.at[tap], out_hbm.at[tap], sems.at[tap]))
            copies[-1].start()
        for copy in copies:
            copy.wait()

    return pl.pallas_call(
        body,
        out_specs=pl.BlockSpec(memory_space=pltpu.HBM),
        out_shape=jax.ShapeDtypeStruct((9, ob, ib), F32),
        scratch_shapes=[
            pltpu.VMEM((ob, frames * FRAME), BF),
            pltpu.VMEM((3, frames, FRAME + 2 * W, ib), BF),
            pltpu.VMEM((9, ob, ib), F32),
            pltpu.SemaphoreType.DMA((9,)),
        ],
        compiler_params=pltpu.CompilerParams(vmem_limit_bytes=24 * MIB),
        name="spatial_grads",
    )(*grads, *grads_sibling, *fields, *fields_sibling)


def temporal_grads(grads, grads_sibling, fields, fields_sibling, scale):
    _, n_x = sizes()
    ob, ib = grads[0].shape[0], fields[0].shape[0]
    span = FT * n_x * FRAME

    def body(*refs):
        g_refs, gs_refs, h_refs, hs_refs = (refs[q * n_x : (q + 1) * n_x] for q in range(4))
        out_hbm, left, right, out, sems = refs[4 * n_x :]
        _, m, band = place()
        right[:FRAME, :] = jnp.zeros((FRAME, ib), BF)
        right[FRAME + span :, :] = jnp.zeros((FRAME, ib), BF)
        for j in range(n_x):
            block = (m + n_x - j) % n_x
            for a, frame in enumerate(frames_of(g_refs[j][...], gs_refs[j][...], band)):
                at = pl.multiple_of((FT * block + a) * FRAME, FRAME)
                left[:, pl.ds(at, FRAME)] = frame.astype(BF)
            for a, frame in enumerate(frames_of(h_refs[j][...], hs_refs[j][...], band)):
                at = pl.multiple_of((FT * block + a + 1) * FRAME, FRAME)
                right[pl.ds(at, FRAME), :] = frame.T.astype(BF)
        copies = []
        for d in range(3):
            moved = right[d * FRAME : d * FRAME + span, :]
            out[d] = jnp.dot(left[...], moved, preferred_element_type=F32) * scale
            copies.append(pltpu.make_async_copy(out.at[d], out_hbm.at[d], sems.at[d]))
            copies[-1].start()
        for copy in copies:
            copy.wait()

    return pl.pallas_call(
        body,
        out_specs=pl.BlockSpec(memory_space=pltpu.HBM),
        out_shape=jax.ShapeDtypeStruct((3, ob, ib), F32),
        scratch_shapes=[
            pltpu.VMEM((ob, span), BF),
            pltpu.VMEM((span + 2 * FRAME, ib), BF),
            pltpu.VMEM((3, ob, ib), F32),
            pltpu.SemaphoreType.DMA((3,)),
        ],
        compiler_params=pltpu.CompilerParams(vmem_limit_bytes=24 * MIB),
        name="temporal_grads",
    )(*grads, *grads_sibling, *fields, *fields_sibling)


def scatter_ch(chunks):
    return [send(chunks[k], "ch", k) for k in range(1, len(chunks))]


def total_of(base, own, received):
    total = base.astype(F32) + own
    for chunk in received:
        total = total + chunk.astype(F32)
    return total.astype(BF)


def on_device(latents, spatial_weight, temporal_weight, cotangent):
    n_ch, n_x = sizes()
    assert n_ch == RBANDS * n_x
    c, m, band = place()
    scale = 1.0 / math.sqrt(TILE * RBANDS * n_x)

    def block(pieces, b):
        stack = jnp.stack(pieces) if isinstance(pieces, list) else pieces
        return lax.dynamic_index_in_dim(stack, (c + n_ch - b) % n_ch, 0, keepdims=False)

    own_block = RBANDS * m + band
    sib_block = RBANDS * m + 1 - band

    siblings = [swap_band(latents)]
    mine = gather_ch(latents)
    cot_ring = ring_blocks(cotangent)
    chunks = temporal_backward(cotangent, cot_ring[0], cot_ring[-1], temporal_weight)
    partials = scatter_ch(chunks)
    mine = after_all(mine, chunks)

    siblings += [swap_band(piece) for piece in mine[1:]]
    cots = [cotangent] + cot_ring
    cots_sibling = [swap_band(x) for x in cots]
    siblings = after_all(siblings, cots_sibling)
    lat_own, lat_sib = [block(mine, own_block)], [block(siblings, own_block)]
    for j in range(1, n_x):
        target = RBANDS * ((m + j) % n_x) + band
        both = send(jnp.stack([block(mine, target), block(siblings, target)]), "st", RBANDS * j)
        lat_own.append(both[0])
        lat_sib.append(both[1])
    hidden = spatial_forward(mine, siblings, spatial_weight)
    hidden_mine = gather_ch(hidden)

    hidden_grad = total_of(after_all(cotangent, hidden), chunks[0], partials)
    grad_ring = ring_blocks(hidden_grad)
    grad_sibling = swap_band(hidden_grad)
    chunks = spatial_backward(hidden_grad, grad_sibling, spatial_weight)
    partials = scatter_ch(chunks)

    grads = [hidden_grad] + grad_ring
    grads_sibling = [grad_sibling] + [swap_band(x) for x in grad_ring]
    lat_own = after_all(lat_own, partials[0])
    spatial_grad = spatial_grads(grads, grads_sibling, lat_own, lat_sib, scale)

    hidden_mine = after_all(hidden_mine, chunks)
    before, after = neighbours(jnp.stack(hidden_mine))
    before, after = after_all((before, after), (spatial_grad, partials[1]))
    temporal_out = temporal_forward(hidden_mine, before, after, temporal_weight)

    hid_own, hid_sib = [block(hidden_mine, own_block)], [block(hidden_mine, sib_block)]
    for j in range(1, n_x):
        if n_x == 2:
            hid_own.append(block(before, own_block))
            hid_sib.append(block(before, sib_block))
        else:
            target = RBANDS * ((m + j) % n_x)
            both = jnp.stack([block(hidden_mine, target + band), block(hidden_mine, target + 1 - band)])
            both = send(both, "st", RBANDS * j)
            hid_own.append(both[0])
            hid_sib.append(both[1])
    hid_own = after_all(hid_own, partials[2:])
    temporal_grad = temporal_grads(cots, cots_sibling, hid_own, [swap_band(x) for x in hid_sib], scale)

    latent_grad = total_of(hidden_grad, chunks[0], partials)
    return temporal_out, latent_grad, spatial_grad, temporal_grad


def solution(mesh):
    return jax.shard_map(
        on_device,
        mesh=mesh,
        in_specs=(
            P("ch", ("groups", "st")),
            P(None, "ch", None),
            P(None, "ch", None),
            P("ch", ("groups", "st")),
        ),
        out_specs=(
            P("ch", ("groups", "st")),
            P("ch", ("groups", "st")),
            P("groups", "ch", "st"),
            P("groups", "ch", "st"),
        ),
        check_vma=False,
    )
```

```python
import math

import jax
import jax.numpy as jnp
from jax import lax
from jax.experimental import pallas as pl
from jax.experimental.pallas import tpu as pltpu
from jax.sharding import PartitionSpec as P

FT = 2
RT = 2
W = 32
RBANDS = 2
TILE = FT * RT * W
HALF = RT * W
ROWS = RBANDS * RT
FRAME = ROWS * W
MIB = 1 << 20
BF = jnp.bfloat16
F32 = jnp.float32


def sizes():
    return lax.axis_size("ch"), lax.axis_size("st") // RBANDS


def place():
    st = lax.axis_index("st")
    return lax.axis_index("ch"), st // RBANDS, st % RBANDS


def send(data, axis, by):
    n = lax.axis_size(axis)
    return lax.ppermute(data, axis, [(i, (i + by) % n) for i in range(n)])


def swap_ch(data, k):
    return lax.ppermute(data, "ch", [(i, i ^ k) for i in range(lax.axis_size("ch"))])


def swap_band(data):
    n = lax.axis_size("st")
    return lax.ppermute(data, "st", [(i, i ^ 1) for i in range(n)])


def after_all(values, others):
    return lax.optimization_barrier((values, others))[0]


def gather_ch(shard):
    n_ch, _ = sizes()
    return [shard] + [swap_ch(shard, k) for k in range(1, n_ch)]


def ring_blocks(data):
    _, n_x = sizes()
    return [send(data, "st", RBANDS * j) for j in range(1, n_x)]


def neighbours(data):
    _, n_x = sizes()
    if n_x == 2:
        other = send(data, "st", RBANDS)
        return other, other
    return send(data, "st", RBANDS), send(data, "st", -RBANDS)


def lanes(shape):
    return lax.broadcasted_iota(jnp.int32, shape, len(shape) - 1)


def roll(x, by):
    return pltpu.roll(x, by, x.ndim - 1)


def frames_of(own, sibling, band):
    own = own.astype(F32)
    sibling = sibling.astype(F32)
    first = jnp.where(band == 0, own, sibling)
    second = jnp.where(band == 0, sibling, own)
    low = lanes(first.shape) < HALF
    return jnp.where(low, first, roll(second, HALF)), jnp.where(low, roll(first, HALF), second)


def tile_of(frame0, frame1, band):
    low = lanes(frame0.shape) < HALF
    upper = jnp.where(low, frame0, roll(frame1, HALF))
    lower = jnp.where(low, roll(frame0, HALF), frame1)
    return jnp.where(band == 0, upper, lower)


def time_pieces(own, before, after, m, n_x):
    own32 = own.astype(F32)
    before = jnp.where(m > 0, before.astype(F32), 0.0)
    after = jnp.where(m < n_x - 1, after.astype(F32), 0.0)
    low = lanes(own32.shape) < HALF
    earlier = roll(jnp.where(low, own32, before), HALF)
    later = roll(jnp.where(low, after, own32), HALF)
    return earlier.astype(BF), own, later.astype(BF)


def inside(dr, dc, shape):
    lane = lanes(shape)
    row = lane // W + dr
    col = lane % W + dc
    return (row >= 0) & (row < ROWS) & (col >= 0) & (col < W)


def spatial_forward(mine, siblings, weight):
    n_ch, n_x = sizes()
    cb = mine[0].shape[0]
    channels = n_ch * cb

    def body(*refs):
        mine_refs, sibling_refs = refs[:n_ch], refs[n_ch : 2 * n_ch]
        w_ref, out_ref, field, acc = refs[2 * n_ch :]
        c, _, band = place()
        for k in range(n_ch):
            at = pl.ds(pl.multiple_of((c ^ k) * cb, 16), cb)
            f0, f1 = frames_of(mine_refs[k][...], sibling_refs[k][...], band)
            field[at, :FRAME] = f0.astype(BF)
            field[at, FRAME:] = f1.astype(BF)
        for tap in range(9):
            dr, dc = tap // 3 - 1, tap % 3 - 1
            part = jnp.dot(w_ref[tap], field[...], preferred_element_type=F32)
            by = (-(W * dr + dc)) % FRAME
            ok = inside(dr, dc, (cb, FRAME))
            for a in range(FT):
                at = slice(a * FRAME, (a + 1) * FRAME)
                moved = part[:, at]
                if by:
                    moved = jnp.where(ok, roll(moved, by), 0.0)
                acc[:, at] = moved + acc[:, at] if tap else moved
        total = tile_of(acc[:, :FRAME], acc[:, FRAME:], band)
        out_ref[...] = (mine_refs[0][...].astype(F32) + total).astype(BF)

    return pl.pallas_call(
        body,
        out_shape=jax.ShapeDtypeStruct((cb, TILE), BF),
        scratch_shapes=[pltpu.VMEM((channels, FT * FRAME), BF), pltpu.VMEM((cb, FT * FRAME), F32)],
        compiler_params=pltpu.CompilerParams(vmem_limit_bytes=16 * MIB),
        name="spatial_forward",
    )(*mine, *siblings, weight)


def temporal_forward(mine, before, after, weight):
    n_ch, n_x = sizes()
    cb = mine[0].shape[0]
    channels = n_ch * cb

    def body(*refs):
        mine_refs = refs[:n_ch]
        before_ref, after_ref, w_ref, out_ref, field = refs[n_ch:]
        c, m, _ = place()
        for k in range(n_ch):
            at = pl.ds(pl.multiple_of((c ^ k) * cb, 16), cb)
            pieces = time_pieces(mine_refs[k][...], before_ref[k], after_ref[k], m, n_x)
            for d in range(3):
                field[d, at, :] = pieces[d]
        total = mine_refs[0][...].astype(F32)
        for d in range(3):
            total += jnp.dot(w_ref[d], field[d], preferred_element_type=F32)
        out_ref[...] = total.astype(BF)

    return pl.pallas_call(
        body,
        out_shape=jax.ShapeDtypeStruct((cb, TILE), BF),
        scratch_shapes=[pltpu.VMEM((3, channels, TILE), BF)],
        compiler_params=pltpu.CompilerParams(vmem_limit_bytes=16 * MIB),
        name="temporal_forward",
    )(*mine, before, after, weight)


def emit_chunks(total, scratch, out_refs, c, n_ch, cb):
    scratch[...] = total.T
    for k in range(n_ch):
        at = pl.ds(pl.multiple_of((c ^ k) * cb, 16), cb)
        out_refs[k][...] = scratch[at, :].astype(out_refs[k].dtype)


def chunk_shapes(n_ch, cb):
    return [jax.ShapeDtypeStruct((cb, TILE), BF if k else F32) for k in range(n_ch)]


def temporal_backward(field, before, after, weight):
    n_ch, n_x = sizes()
    cb = field.shape[0]
    channels = n_ch * cb

    def body(field_hbm, before_ref, after_ref, w_hbm, *rest):
        out_refs, (field_ref, w_ref, scratch, sems) = rest[:n_ch], rest[n_ch:]
        first = pltpu.make_async_copy(field_hbm, field_ref, sems.at[3])
        first.start()
        copies = [pltpu.make_async_copy(w_hbm.at[d], w_ref.at[d], sems.at[d]) for d in range(3)]
        for copy in copies:
            copy.start()
        c, m, _ = place()
        first.wait()
        pieces = time_pieces(field_ref[...], before_ref[...], after_ref[...], m, n_x)
        total = jnp.zeros((TILE, channels), F32)
        for d in range(3):
            left = pieces[2 - d].astype(F32).T.astype(BF)
            copies[d].wait()
            total += jnp.dot(left, w_ref[d], preferred_element_type=F32)
        emit_chunks(total, scratch, out_refs, c, n_ch, cb)

    vmem = pl.BlockSpec(memory_space=pltpu.VMEM)
    hbm = pl.BlockSpec(memory_space=pltpu.HBM)
    in_hbm = lambda x: pltpu.with_memory_space_constraint(x, pltpu.HBM)
    return pl.pallas_call(
        body,
        in_specs=[hbm, vmem, vmem, hbm],
        out_specs=[vmem] * n_ch,
        out_shape=chunk_shapes(n_ch, cb),
        scratch_shapes=[
            pltpu.VMEM(field.shape, BF),
            pltpu.VMEM(weight.shape, BF),
            pltpu.VMEM((channels, TILE), F32),
            pltpu.SemaphoreType.DMA((4,)),
        ],
        compiler_params=pltpu.CompilerParams(vmem_limit_bytes=16 * MIB),
        cost_estimate=pl.CostEstimate(flops=4_000_000_000, transcendentals=0, bytes_accessed=3_000_000),
        name="temporal_backward",
    )(in_hbm(field), before, after, in_hbm(weight))


def shifted_columns(frame, toward):
    cells = frame.T
    col = lax.broadcasted_iota(jnp.int32, cells.shape, 0) % W
    out = []
    for dc in (-toward, 0, toward):
        moved = cells
        if dc:
            ok = (col + dc >= 0) & (col + dc < W)
            moved = jnp.where(ok, pltpu.roll(cells, (-dc) % FRAME, 0), 0.0)
        out.append(moved.astype(BF))
    return out


def spatial_backward(field, sibling, weight):
    n_ch, _ = sizes()
    cb = field.shape[0]
    channels = n_ch * cb

    def body(field_ref, sibling_ref, w_ref, *rest):
        out_refs, (left, scratch) = rest[:n_ch], rest[n_ch:]
        c, _, band = place()
        blank = jnp.zeros((W, 3 * cb), BF)
        for a, frame in enumerate(frames_of(field_ref[...], sibling_ref[...], band)):
            left[a, :W, :] = blank
            left[a, W + FRAME :, :] = blank
            for q, moved in enumerate(shifted_columns(frame, -1)):
                left[a, W : W + FRAME, q * cb : (q + 1) * cb] = moved
        total = jnp.zeros((TILE, channels), F32)
        for g in range(3):
            start = pl.multiple_of(HALF * band + W * (2 - g), W)
            rows = jnp.concatenate([left[a, pl.ds(start, HALF), :] for a in range(FT)], axis=0)
            total += jnp.dot(rows, w_ref[g], preferred_element_type=F32)
        emit_chunks(total, scratch, out_refs, c, n_ch, cb)

    return pl.pallas_call(
        body,
        out_shape=chunk_shapes(n_ch, cb),
        scratch_shapes=[
            pltpu.VMEM((FT, FRAME + 2 * W, 3 * cb), BF),
            pltpu.VMEM((channels, TILE), F32),
        ],
        compiler_params=pltpu.CompilerParams(vmem_limit_bytes=16 * MIB),
        name="spatial_backward",
    )(field, sibling, weight.reshape(3, 3 * cb, channels))


def spatial_grads(grads, grads_sibling, fields, fields_sibling, scale):
    _, n_x = sizes()
    ob, ib = grads[0].shape[0], fields[0].shape[0]
    frames = FT * n_x

    def body(*refs):
        g_refs, gs_refs, l_refs, ls_refs = (refs[q * n_x : (q + 1) * n_x] for q in range(4))
        out_hbm, left, right, out, sems = refs[4 * n_x :]
        _, _, band = place()
        blank = jnp.zeros((W, ib), BF)
        for j in range(n_x):
            for a, frame in enumerate(frames_of(g_refs[j][...], gs_refs[j][...], band)):
                f = FT * j + a
                left[:, f * FRAME : (f + 1) * FRAME] = frame.astype(BF)
            for a, frame in enumerate(frames_of(l_refs[j][...], ls_refs[j][...], band)):
                f = FT * j + a
                for q, moved in enumerate(shifted_columns(frame, 1)):
                    right[q, f, :W, :] = blank
                    right[q, f, W + FRAME :, :] = blank
                    right[q, f, W : W + FRAME, :] = moved
        copies = []
        for tap in range(9):
            at = slice(W * (tap // 3), W * (tap // 3) + FRAME)
            moved = jnp.concatenate([right[tap % 3, f, at, :] for f in range(frames)], axis=0)
            out[tap] = jnp.dot(left[...], moved, preferred_element_type=F32) * scale
            copies.append(pltpu.make_async_copy(out.at[tap], out_hbm.at[tap], sems.at[tap]))
            copies[-1].start()
        for copy in copies:
            copy.wait()

    return pl.pallas_call(
        body,
        out_specs=pl.BlockSpec(memory_space=pltpu.HBM),
        out_shape=jax.ShapeDtypeStruct((9, ob, ib), F32),
        scratch_shapes=[
            pltpu.VMEM((ob, frames * FRAME), BF),
            pltpu.VMEM((3, frames, FRAME + 2 * W, ib), BF),
            pltpu.VMEM((9, ob, ib), F32),
            pltpu.SemaphoreType.DMA((9,)),
        ],
        compiler_params=pltpu.CompilerParams(vmem_limit_bytes=24 * MIB),
        name="spatial_grads",
    )(*grads, *grads_sibling, *fields, *fields_sibling)


def temporal_grads(grads, grads_sibling, fields, fields_sibling, scale):
    _, n_x = sizes()
    ob, ib = grads[0].shape[0], fields[0].shape[0]
    span = FT * n_x * FRAME

    def body(*refs):
        g_refs, gs_refs, h_refs, hs_refs = (refs[q * n_x : (q + 1) * n_x] for q in range(4))
        out_hbm, left, right, out, sems = refs[4 * n_x :]
        _, m, band = place()
        right[:FRAME, :] = jnp.zeros((FRAME, ib), BF)
        right[FRAME + span :, :] = jnp.zeros((FRAME, ib), BF)
        for j in range(n_x):
            block = (m + n_x - j) % n_x
            for a, frame in enumerate(frames_of(g_refs[j][...], gs_refs[j][...], band)):
                at = pl.multiple_of((FT * block + a) * FRAME, FRAME)
                left[:, pl.ds(at, FRAME)] = frame.astype(BF)
            for a, frame in enumerate(frames_of(h_refs[j][...], hs_refs[j][...], band)):
                at = pl.multiple_of((FT * block + a + 1) * FRAME, FRAME)
                right[pl.ds(at, FRAME), :] = frame.T.astype(BF)
        copies = []
        for d in range(3):
            moved = right[d * FRAME : d * FRAME + span, :]
            out[d] = jnp.dot(left[...], moved, preferred_element_type=F32) * scale
            copies.append(pltpu.make_async_copy(out.at[d], out_hbm.at[d], sems.at[d]))
            copies[-1].start()
        for copy in copies:
            copy.wait()

    return pl.pallas_call(
        body,
        out_specs=pl.BlockSpec(memory_space=pltpu.HBM),
        out_shape=jax.ShapeDtypeStruct((3, ob, ib), F32),
        scratch_shapes=[
            pltpu.VMEM((ob, span), BF),
            pltpu.VMEM((span + 2 * FRAME, ib), BF),
            pltpu.VMEM((3, ob, ib), F32),
            pltpu.SemaphoreType.DMA((3,)),
        ],
        compiler_params=pltpu.CompilerParams(vmem_limit_bytes=24 * MIB),
        name="temporal_grads",
    )(*grads, *grads_sibling, *fields, *fields_sibling)


def scatter_ch(chunks):
    return [swap_ch(chunks[k], k) for k in range(1, len(chunks))]


def total_of(base, own, received):
    total = base.astype(F32) + own
    for chunk in received:
        total = total + chunk.astype(F32)
    return total.astype(BF)


def on_device(latents, spatial_weight, temporal_weight, cotangent):
    n_ch, n_x = sizes()
    assert n_ch == RBANDS * n_x and n_ch & (n_ch - 1) == 0
    c, m, band = place()
    scale = 1.0 / math.sqrt(TILE * RBANDS * n_x)

    def block(pieces, b):
        stack = jnp.stack(pieces) if isinstance(pieces, list) else pieces
        return lax.dynamic_index_in_dim(stack, c ^ b, 0, keepdims=False)

    own_block = RBANDS * m + band
    sib_block = RBANDS * m + 1 - band

    siblings = [swap_band(latents)]
    mine = gather_ch(latents)
    cot_ring = ring_blocks(cotangent)
    chunks = temporal_backward(cotangent, cot_ring[0], cot_ring[-1], temporal_weight)
    partials = scatter_ch(chunks)
    mine = after_all(mine, chunks)

    siblings += [swap_band(piece) for piece in mine[1:]]
    cots = [cotangent] + cot_ring
    cots_sibling = [swap_band(x) for x in cots]
    siblings = after_all(siblings, cots_sibling)
    lat_own, lat_sib = [block(mine, own_block)], [block(siblings, own_block)]
    for j in range(1, n_x):
        target = RBANDS * ((m + j) % n_x) + band
        both = send(jnp.stack([block(mine, target), block(siblings, target)]), "st", RBANDS * j)
        lat_own.append(both[0])
        lat_sib.append(both[1])
    hidden = spatial_forward(mine, siblings, spatial_weight)
    hidden_mine = gather_ch(hidden)

    hidden_grad = total_of(after_all(cotangent, hidden), chunks[0], partials)
    grad_ring = ring_blocks(hidden_grad)
    grad_sibling = swap_band(hidden_grad)
    chunks = spatial_backward(hidden_grad, grad_sibling, spatial_weight)
    partials = scatter_ch(chunks)

    grads = [hidden_grad] + grad_ring
    grads_sibling = [grad_sibling] + [swap_band(x) for x in grad_ring]
    lat_own = after_all(lat_own, partials[0])
    spatial_grad = spatial_grads(grads, grads_sibling, lat_own, lat_sib, scale)

    hidden_mine = after_all(hidden_mine, chunks)
    before, after = neighbours(jnp.stack(hidden_mine))
    before, after = after_all((before, after), (spatial_grad, partials[1]))
    temporal_out = temporal_forward(hidden_mine, before, after, temporal_weight)

    hid_own, hid_sib = [block(hidden_mine, own_block)], [block(hidden_mine, sib_block)]
    for j in range(1, n_x):
        if n_x == 2:
            hid_own.append(block(before, own_block))
            hid_sib.append(block(before, sib_block))
        else:
            target = RBANDS * ((m + j) % n_x)
            both = jnp.stack([block(hidden_mine, target + band), block(hidden_mine, target + 1 - band)])
            both = send(both, "st", RBANDS * j)
            hid_own.append(both[0])
            hid_sib.append(both[1])
    hid_own = after_all(hid_own, partials[2:])
    temporal_grad = temporal_grads(cots, cots_sibling, hid_own, [swap_band(x) for x in hid_sib], scale)

    latent_grad = total_of(hidden_grad, chunks[0], partials)
    return temporal_out, latent_grad, spatial_grad, temporal_grad


def solution(mesh):
    return jax.shard_map(
        on_device,
        mesh=mesh,
        in_specs=(
            P("ch", ("groups", "st")),
            P(None, "ch", None),
            P(None, "ch", None),
            P("ch", ("groups", "st")),
        ),
        out_specs=(
            P("ch", ("groups", "st")),
            P("ch", ("groups", "st")),
            P("groups", "ch", "st"),
            P("groups", "ch", "st"),
        ),
        check_vma=False,
    )
```

```python
import math

import jax
import jax.numpy as jnp
from jax import lax
from jax.experimental import pallas as pl
from jax.experimental.pallas import tpu as pltpu
from jax.sharding import PartitionSpec as P

FT = 2
RT = 2
W = 32
RBANDS = 2
TILE = FT * RT * W
HALF = RT * W
ROWS = RBANDS * RT
FRAME = ROWS * W
MIB = 1 << 20
BF = jnp.bfloat16
F32 = jnp.float32


def sizes():
    return lax.axis_size("ch"), lax.axis_size("st") // RBANDS


def place():
    st = lax.axis_index("st")
    return lax.axis_index("ch"), st // RBANDS, st % RBANDS


def send(data, axis, by):
    n = lax.axis_size(axis)
    return lax.ppermute(data, axis, [(i, (i + by) % n) for i in range(n)])


def swap_band(data):
    n = lax.axis_size("st")
    return lax.ppermute(data, "st", [(i, i ^ 1) for i in range(n)])


def after_all(values, others):
    return lax.optimization_barrier((values, others))[0]


def gather_ch(shard):
    n_ch, _ = sizes()
    return [shard] + [send(shard, "ch", k) for k in range(1, n_ch)]


def ring_blocks(data):
    _, n_x = sizes()
    return [send(data, "st", RBANDS * j) for j in range(1, n_x)]


def neighbours(data):
    _, n_x = sizes()
    if n_x == 2:
        other = send(data, "st", RBANDS)
        return other, other
    return send(data, "st", RBANDS), send(data, "st", -RBANDS)


def lanes(shape):
    return lax.broadcasted_iota(jnp.int32, shape, len(shape) - 1)


def roll(x, by):
    return pltpu.roll(x, by, x.ndim - 1)


def frames_of(own, sibling, band):
    own = own.astype(F32)
    sibling = sibling.astype(F32)
    first = jnp.where(band == 0, own, sibling)
    second = jnp.where(band == 0, sibling, own)
    low = lanes(first.shape) < HALF
    return jnp.where(low, first, roll(second, HALF)), jnp.where(low, roll(first, HALF), second)


def tile_of(frame0, frame1, band):
    low = lanes(frame0.shape) < HALF
    upper = jnp.where(low, frame0, roll(frame1, HALF))
    lower = jnp.where(low, roll(frame0, HALF), frame1)
    return jnp.where(band == 0, upper, lower)


def time_pieces(own, before, after, m, n_x):
    own32 = own.astype(F32)
    before = jnp.where(m > 0, before.astype(F32), 0.0)
    after = jnp.where(m < n_x - 1, after.astype(F32), 0.0)
    low = lanes(own32.shape) < HALF
    earlier = roll(jnp.where(low, own32, before), HALF)
    later = roll(jnp.where(low, after, own32), HALF)
    return earlier.astype(BF), own, later.astype(BF)


def inside(dr, dc, shape):
    lane = lanes(shape)
    row = lane // W + dr
    col = lane % W + dc
    return (row >= 0) & (row < ROWS) & (col >= 0) & (col < W)


def spatial_forward(mine, siblings, weight):
    n_ch, n_x = sizes()
    cb = mine[0].shape[0]
    channels = n_ch * cb

    def body(*refs):
        mine_refs, sibling_refs = refs[:n_ch], refs[n_ch : 2 * n_ch]
        w_ref, out_ref, field, acc = refs[2 * n_ch :]
        c, _, band = place()
        for k in range(n_ch):
            at = pl.ds(pl.multiple_of(((c + n_ch - k) % n_ch) * cb, 16), cb)
            f0, f1 = frames_of(mine_refs[k][...], sibling_refs[k][...], band)
            field[at, :FRAME] = f0.astype(BF)
            field[at, FRAME:] = f1.astype(BF)
        for tap in range(9):
            dr, dc = tap // 3 - 1, tap % 3 - 1
            part = jnp.dot(w_ref[tap], field[...], preferred_element_type=F32)
            by = (-(W * dr + dc)) % FRAME
            ok = inside(dr, dc, (cb, FRAME))
            for a in range(FT):
                at = slice(a * FRAME, (a + 1) * FRAME)
                moved = part[:, at]
                if by:
                    moved = jnp.where(ok, roll(moved, by), 0.0)
                acc[:, at] = moved + acc[:, at] if tap else moved
        total = tile_of(acc[:, :FRAME], acc[:, FRAME:], band)
        out_ref[...] = (mine_refs[0][...].astype(F32) + total).astype(BF)

    return pl.pallas_call(
        body,
        out_shape=jax.ShapeDtypeStruct((cb, TILE), BF),
        scratch_shapes=[pltpu.VMEM((channels, FT * FRAME), BF), pltpu.VMEM((cb, FT * FRAME), F32)],
        compiler_params=pltpu.CompilerParams(vmem_limit_bytes=16 * MIB),
        name="spatial_forward",
    )(*mine, *siblings, weight)


def temporal_forward(mine, before, after, weight):
    n_ch, n_x = sizes()
    cb = mine[0].shape[0]
    channels = n_ch * cb

    def body(*refs):
        mine_refs = refs[:n_ch]
        before_ref, after_ref, w_ref, out_ref, field = refs[n_ch:]
        c, m, _ = place()
        for k in range(n_ch):
            at = pl.ds(pl.multiple_of(((c + n_ch - k) % n_ch) * cb, 16), cb)
            pieces = time_pieces(mine_refs[k][...], before_ref[k], after_ref[k], m, n_x)
            for d in range(3):
                field[d, at, :] = pieces[d]
        total = mine_refs[0][...].astype(F32)
        for d in range(3):
            total += jnp.dot(w_ref[d], field[d], preferred_element_type=F32)
        out_ref[...] = total.astype(BF)

    return pl.pallas_call(
        body,
        out_shape=jax.ShapeDtypeStruct((cb, TILE), BF),
        scratch_shapes=[pltpu.VMEM((3, channels, TILE), BF)],
        compiler_params=pltpu.CompilerParams(vmem_limit_bytes=16 * MIB),
        name="temporal_forward",
    )(*mine, before, after, weight)


def emit_chunks(total, scratch, out_refs, c, n_ch, cb):
    scratch[...] = total.T
    for k in range(n_ch):
        at = pl.ds(pl.multiple_of(((c + k) % n_ch) * cb, 16), cb)
        out_refs[k][...] = scratch[at, :].astype(out_refs[k].dtype)


def chunk_shapes(n_ch, cb):
    return [jax.ShapeDtypeStruct((cb, TILE), BF if k else F32) for k in range(n_ch)]


def temporal_backward(ring, weight):
    n_ch, n_x = sizes()
    field = ring[0]
    cb = field.shape[0]
    channels = n_ch * cb

    def body(*refs):
        ring_refs, w_ref, out_refs = refs[:n_x], refs[n_x], refs[n_x + 1 : n_x + 1 + n_ch]
        stack_ref, scratch = refs[n_x + 1 + n_ch :]
        field_ref, before_ref, after_ref = ring_refs[0], ring_refs[1], ring_refs[-1]
        c, m, _ = place()
        for j in range(n_x):
            stack_ref[j] = ring_refs[j][...]
        pieces = time_pieces(field_ref[...], before_ref[...], after_ref[...], m, n_x)
        total = jnp.zeros((TILE, channels), F32)
        for d in range(3):
            left = pieces[2 - d].astype(F32).T.astype(BF)
            total += jnp.dot(left, w_ref[d], preferred_element_type=F32)
        emit_chunks(total, scratch, out_refs, c, n_ch, cb)

    *chunks, stack = pl.pallas_call(
        body,
        out_shape=chunk_shapes(n_ch, cb) + [jax.ShapeDtypeStruct((n_x, cb, TILE), BF)],
        scratch_shapes=[pltpu.VMEM((channels, TILE), F32)],
        compiler_params=pltpu.CompilerParams(vmem_limit_bytes=16 * MIB),
        cost_estimate=pl.CostEstimate(flops=2000000000, transcendentals=0, bytes_accessed=3_000_000),
        name="temporal_backward",
    )(*ring, weight)
    return chunks, stack


def shifted_columns(frame, toward):
    cells = frame.T
    col = lax.broadcasted_iota(jnp.int32, cells.shape, 0) % W
    out = []
    for dc in (-toward, 0, toward):
        moved = cells
        if dc:
            ok = (col + dc >= 0) & (col + dc < W)
            moved = jnp.where(ok, pltpu.roll(cells, (-dc) % FRAME, 0), 0.0)
        out.append(moved.astype(BF))
    return out


def spatial_backward(field, sibling, weight):
    n_ch, _ = sizes()
    cb = field.shape[0]
    channels = n_ch * cb

    def body(field_ref, sibling_ref, w_ref, *rest):
        out_refs, (left, scratch) = rest[:n_ch], rest[n_ch:]
        c, _, band = place()
        blank = jnp.zeros((W, 3 * cb), BF)
        for a, frame in enumerate(frames_of(field_ref[...], sibling_ref[...], band)):
            left[a, :W, :] = blank
            left[a, W + FRAME :, :] = blank
            for q, moved in enumerate(shifted_columns(frame, -1)):
                left[a, W : W + FRAME, q * cb : (q + 1) * cb] = moved
        total = jnp.zeros((TILE, channels), F32)
        for g in range(3):
            start = pl.multiple_of(HALF * band + W * (2 - g), W)
            rows = jnp.concatenate([left[a, pl.ds(start, HALF), :] for a in range(FT)], axis=0)
            total += jnp.dot(rows, w_ref[g], preferred_element_type=F32)
        emit_chunks(total, scratch, out_refs, c, n_ch, cb)

    return pl.pallas_call(
        body,
        out_shape=chunk_shapes(n_ch, cb),
        scratch_shapes=[
            pltpu.VMEM((FT, FRAME + 2 * W, 3 * cb), BF),
            pltpu.VMEM((channels, TILE), F32),
        ],
        compiler_params=pltpu.CompilerParams(vmem_limit_bytes=16 * MIB),
        name="spatial_backward",
    )(field, sibling, weight.reshape(3, 3 * cb, channels))


def spatial_grads(grads, grads_sibling, fields, fields_sibling, scale):
    _, n_x = sizes()
    ob, ib = grads[0].shape[0], fields[0].shape[0]
    frames = FT * n_x

    def body(*refs):
        g_refs, gs_refs, l_refs, ls_refs = (refs[q * n_x : (q + 1) * n_x] for q in range(4))
        out_hbm, left, right, out, sems = refs[4 * n_x :]
        _, _, band = place()
        blank = jnp.zeros((W, ib), BF)
        for j in range(n_x):
            for a, frame in enumerate(frames_of(g_refs[j][...], gs_refs[j][...], band)):
                f = FT * j + a
                left[:, f * FRAME : (f + 1) * FRAME] = frame.astype(BF)
            for a, frame in enumerate(frames_of(l_refs[j][...], ls_refs[j][...], band)):
                f = FT * j + a
                for q, moved in enumerate(shifted_columns(frame, 1)):
                    right[q, f, :W, :] = blank
                    right[q, f, W + FRAME :, :] = blank
                    right[q, f, W : W + FRAME, :] = moved
        copies = []
        for tap in range(9):
            at = slice(W * (tap // 3), W * (tap // 3) + FRAME)
            moved = jnp.concatenate([right[tap % 3, f, at, :] for f in range(frames)], axis=0)
            out[tap] = jnp.dot(left[...], moved, preferred_element_type=F32) * scale
            copies.append(pltpu.make_async_copy(out.at[tap], out_hbm.at[tap], sems.at[tap]))
            copies[-1].start()
        for copy in copies:
            copy.wait()

    return pl.pallas_call(
        body,
        out_specs=pl.BlockSpec(memory_space=pltpu.HBM),
        out_shape=jax.ShapeDtypeStruct((9, ob, ib), F32),
        scratch_shapes=[
            pltpu.VMEM((ob, frames * FRAME), BF),
            pltpu.VMEM((3, frames, FRAME + 2 * W, ib), BF),
            pltpu.VMEM((9, ob, ib), F32),
            pltpu.SemaphoreType.DMA((9,)),
        ],
        compiler_params=pltpu.CompilerParams(vmem_limit_bytes=24 * MIB),
        name="spatial_grads",
    )(*grads, *grads_sibling, *fields, *fields_sibling)


def temporal_grads(grads, grads_sibling, fields, fields_sibling, scale):
    _, n_x = sizes()
    ob, ib = grads.shape[1], fields[0].shape[0]
    span = FT * n_x * FRAME

    def body(*refs):
        g_ref, gs_ref = refs[:2]
        h_refs, hs_refs = refs[2 : 2 + n_x], refs[2 + n_x : 2 + 2 * n_x]
        out_hbm, left, right, out, sems = refs[2 + 2 * n_x :]
        _, m, band = place()
        right[:FRAME, :] = jnp.zeros((FRAME, ib), BF)
        right[FRAME + span :, :] = jnp.zeros((FRAME, ib), BF)
        for j in range(n_x):
            block = (m + n_x - j) % n_x
            for a, frame in enumerate(frames_of(g_ref[j], gs_ref[j], band)):
                at = pl.multiple_of((FT * block + a) * FRAME, FRAME)
                left[:, pl.ds(at, FRAME)] = frame.astype(BF)
            for a, frame in enumerate(frames_of(h_refs[j][...], hs_refs[j][...], band)):
                at = pl.multiple_of((FT * block + a + 1) * FRAME, FRAME)
                right[pl.ds(at, FRAME), :] = frame.T.astype(BF)
        copies = []
        for d in range(3):
            moved = right[d * FRAME : d * FRAME + span, :]
            out[d] = jnp.dot(left[...], moved, preferred_element_type=F32) * scale
            copies.append(pltpu.make_async_copy(out.at[d], out_hbm.at[d], sems.at[d]))
            copies[-1].start()
        for copy in copies:
            copy.wait()

    return pl.pallas_call(
        body,
        out_specs=pl.BlockSpec(memory_space=pltpu.HBM),
        out_shape=jax.ShapeDtypeStruct((3, ob, ib), F32),
        scratch_shapes=[
            pltpu.VMEM((ob, span), BF),
            pltpu.VMEM((span + 2 * FRAME, ib), BF),
            pltpu.VMEM((3, ob, ib), F32),
            pltpu.SemaphoreType.DMA((3,)),
        ],
        compiler_params=pltpu.CompilerParams(vmem_limit_bytes=24 * MIB),
        name="temporal_grads",
    )(grads, grads_sibling, *fields, *fields_sibling)


def scatter_ch(chunks):
    return [send(chunks[k], "ch", k) for k in range(1, len(chunks))]


def total_of(base, own, received):
    total = base.astype(F32) + own
    for chunk in received:
        total = total + chunk.astype(F32)
    return total.astype(BF)


def on_device(latents, spatial_weight, temporal_weight, cotangent):
    n_ch, n_x = sizes()
    assert n_ch == RBANDS * n_x
    c, m, band = place()
    scale = 1.0 / math.sqrt(TILE * RBANDS * n_x)

    def block(pieces, b):
        stack = jnp.stack(pieces) if isinstance(pieces, list) else pieces
        return lax.dynamic_index_in_dim(stack, (c + n_ch - b) % n_ch, 0, keepdims=False)

    own_block = RBANDS * m + band
    sib_block = RBANDS * m + 1 - band

    siblings = [swap_band(latents)]
    mine = gather_ch(latents)
    cot_ring = ring_blocks(cotangent)
    chunks, cots = temporal_backward([cotangent] + cot_ring, temporal_weight)
    partials = scatter_ch(chunks)
    mine = after_all(mine, chunks)

    siblings += [swap_band(piece) for piece in mine[1:]]
    cots_sibling = swap_band(cots)
    lat_own, lat_sib = [block(mine, own_block)], [block(siblings, own_block)]
    for j in range(1, n_x):
        target = RBANDS * ((m + j) % n_x) + band
        both = send(jnp.stack([block(mine, target), block(siblings, target)]), "st", RBANDS * j)
        lat_own.append(both[0])
        lat_sib.append(both[1])
    hidden = spatial_forward(mine, siblings, spatial_weight)
    hidden_mine = gather_ch(hidden)

    hidden_grad = total_of(after_all(cotangent, hidden), chunks[0], partials)
    grad_ring = ring_blocks(hidden_grad)
    grad_sibling = swap_band(hidden_grad)
    chunks = spatial_backward(hidden_grad, grad_sibling, spatial_weight)
    partials = scatter_ch(chunks)

    grads = [hidden_grad] + grad_ring
    grads_sibling = [grad_sibling] + [swap_band(x) for x in grad_ring]
    lat_own = after_all(lat_own, partials[0])
    spatial_grad = spatial_grads(grads, grads_sibling, lat_own, lat_sib, scale)

    hidden_mine = after_all(hidden_mine, chunks)
    before, after = neighbours(jnp.stack(hidden_mine))
    before, after = after_all((before, after), (spatial_grad, partials[1]))
    temporal_out = temporal_forward(hidden_mine, before, after, temporal_weight)

    hid_own, hid_sib = [block(hidden_mine, own_block)], [block(hidden_mine, sib_block)]
    for j in range(1, n_x):
        if n_x == 2:
            hid_own.append(block(before, own_block))
            hid_sib.append(block(before, sib_block))
        else:
            target = RBANDS * ((m + j) % n_x)
            both = jnp.stack([block(hidden_mine, target + band), block(hidden_mine, target + 1 - band)])
            both = send(both, "st", RBANDS * j)
            hid_own.append(both[0])
            hid_sib.append(both[1])
    hid_own = after_all(hid_own, partials[2:])
    temporal_grad = temporal_grads(cots, cots_sibling, hid_own, [swap_band(x) for x in hid_sib], scale)

    latent_grad = total_of(hidden_grad, chunks[0], partials)
    return temporal_out, latent_grad, spatial_grad, temporal_grad


def solution(mesh):
    return jax.shard_map(
        on_device,
        mesh=mesh,
        in_specs=(
            P("ch", ("groups", "st")),
            P(None, "ch", None),
            P(None, "ch", None),
            P("ch", ("groups", "st")),
        ),
        out_specs=(
            P("ch", ("groups", "st")),
            P("ch", ("groups", "st")),
            P("groups", "ch", "st"),
            P("groups", "ch", "st"),
        ),
        check_vma=False,
    )
```

```python
import math

import jax
import jax.numpy as jnp
from jax import lax
from jax.experimental import pallas as pl
from jax.experimental.pallas import tpu as pltpu
from jax.sharding import PartitionSpec as P

FT = 2
RT = 2
W = 32
RBANDS = 2
TILE = FT * RT * W
HALF = RT * W
ROWS = RBANDS * RT
FRAME = ROWS * W
MIB = 1 << 20
BF = jnp.bfloat16
F32 = jnp.float32


def sizes():
    return lax.axis_size("ch"), lax.axis_size("st") // RBANDS


def place():
    st = lax.axis_index("st")
    return lax.axis_index("ch"), st // RBANDS, st % RBANDS


def send(data, axis, by):
    n = lax.axis_size(axis)
    return lax.ppermute(data, axis, [(i, (i + by) % n) for i in range(n)])


def swap_band(data):
    n = lax.axis_size("st")
    return lax.ppermute(data, "st", [(i, i ^ 1) for i in range(n)])


def after_all(values, others):
    return lax.optimization_barrier((values, others))[0]


def gather_ch(shard):
    n_ch, _ = sizes()
    return [shard] + [send(shard, "ch", k) for k in range(1, n_ch)]


def ring_blocks(data):
    _, n_x = sizes()
    return [send(data, "st", RBANDS * j) for j in range(1, n_x)]


def neighbours(data):
    _, n_x = sizes()
    if n_x == 2:
        other = send(data, "st", RBANDS)
        return other, other
    return send(data, "st", RBANDS), send(data, "st", -RBANDS)


def lanes(shape):
    return lax.broadcasted_iota(jnp.int32, shape, len(shape) - 1)


def roll(x, by):
    return pltpu.roll(x, by, x.ndim - 1)


def frames_of(own, sibling, band):
    own = own.astype(F32)
    sibling = sibling.astype(F32)
    first = jnp.where(band == 0, own, sibling)
    second = jnp.where(band == 0, sibling, own)
    low = lanes(first.shape) < HALF
    return jnp.where(low, first, roll(second, HALF)), jnp.where(low, roll(first, HALF), second)


def tile_of(frame0, frame1, band):
    low = lanes(frame0.shape) < HALF
    upper = jnp.where(low, frame0, roll(frame1, HALF))
    lower = jnp.where(low, roll(frame0, HALF), frame1)
    return jnp.where(band == 0, upper, lower)


def time_pieces(own, before, after, m, n_x):
    own32 = own.astype(F32)
    before = jnp.where(m > 0, before.astype(F32), 0.0)
    after = jnp.where(m < n_x - 1, after.astype(F32), 0.0)
    low = lanes(own32.shape) < HALF
    earlier = roll(jnp.where(low, own32, before), HALF)
    later = roll(jnp.where(low, after, own32), HALF)
    return earlier.astype(BF), own, later.astype(BF)


def inside(dr, dc, shape):
    lane = lanes(shape)
    row = lane // W + dr
    col = lane % W + dc
    return (row >= 0) & (row < ROWS) & (col >= 0) & (col < W)


def spatial_forward(mine, siblings, weight):
    n_ch, n_x = sizes()
    cb = mine[0].shape[0]
    channels = n_ch * cb

    def body(*refs):
        mine_refs, sibling_refs = refs[:n_ch], refs[n_ch : 2 * n_ch]
        w_ref, out_ref, field, acc = refs[2 * n_ch :]
        c, _, band = place()
        for k in range(n_ch):
            at = pl.ds(pl.multiple_of(((c + n_ch - k) % n_ch) * cb, 16), cb)
            f0, f1 = frames_of(mine_refs[k][...], sibling_refs[k][...], band)
            field[at, :FRAME] = f0.astype(BF)
            field[at, FRAME:] = f1.astype(BF)
        for tap in range(9):
            dr, dc = tap // 3 - 1, tap % 3 - 1
            part = jnp.dot(w_ref[tap], field[...], preferred_element_type=F32)
            by = (-(W * dr + dc)) % FRAME
            ok = inside(dr, dc, (cb, FRAME))
            for a in range(FT):
                at = slice(a * FRAME, (a + 1) * FRAME)
                moved = part[:, at]
                if by:
                    moved = jnp.where(ok, roll(moved, by), 0.0)
                acc[:, at] = moved + acc[:, at] if tap else moved
        total = tile_of(acc[:, :FRAME], acc[:, FRAME:], band)
        out_ref[...] = (mine_refs[0][...].astype(F32) + total).astype(BF)

    return pl.pallas_call(
        body,
        out_shape=jax.ShapeDtypeStruct((cb, TILE), BF),
        scratch_shapes=[pltpu.VMEM((channels, FT * FRAME), BF), pltpu.VMEM((cb, FT * FRAME), F32)],
        compiler_params=pltpu.CompilerParams(vmem_limit_bytes=16 * MIB),
        name="spatial_forward",
    )(*mine, *siblings, weight)


def temporal_forward(mine, before, after, weight):
    n_ch, n_x = sizes()
    cb = mine[0].shape[0]
    channels = n_ch * cb

    def body(*refs):
        mine_refs = refs[:n_ch]
        before_ref, after_ref, w_ref, out_ref, field = refs[n_ch:]
        c, m, _ = place()
        for k in range(n_ch):
            at = pl.ds(pl.multiple_of(((c + n_ch - k) % n_ch) * cb, 16), cb)
            pieces = time_pieces(mine_refs[k][...], before_ref[k], after_ref[k], m, n_x)
            for d in range(3):
                field[d, at, :] = pieces[d]
        total = mine_refs[0][...].astype(F32)
        for d in range(3):
            total += jnp.dot(w_ref[d], field[d], preferred_element_type=F32)
        out_ref[...] = total.astype(BF)

    return pl.pallas_call(
        body,
        out_shape=jax.ShapeDtypeStruct((cb, TILE), BF),
        scratch_shapes=[pltpu.VMEM((3, channels, TILE), BF)],
        compiler_params=pltpu.CompilerParams(vmem_limit_bytes=16 * MIB),
        name="temporal_forward",
    )(*mine, before, after, weight)


def emit_chunks(total, scratch, out_refs, c, n_ch, cb):
    scratch[...] = total.T
    for k in range(n_ch):
        at = pl.ds(pl.multiple_of(((c + k) % n_ch) * cb, 16), cb)
        out_refs[k][...] = scratch[at, :].astype(out_refs[k].dtype)


def chunk_shapes(n_ch, cb):
    return [jax.ShapeDtypeStruct((cb, TILE), BF if k else F32) for k in range(n_ch)]


def temporal_backward(ring, weight):
    n_ch, n_x = sizes()
    field = ring[0]
    cb = field.shape[0]
    channels = n_ch * cb

    def body(*refs):
        ring_refs, w_ref, out_refs = refs[:n_x], refs[n_x], refs[n_x + 1 : n_x + 1 + n_ch]
        stack_ref, scratch = refs[n_x + 1 + n_ch :]
        field_ref, before_ref, after_ref = ring_refs[0], ring_refs[1], ring_refs[-1]
        c, m, _ = place()
        for j in range(n_x):
            stack_ref[j] = ring_refs[j][...]
        pieces = time_pieces(field_ref[...], before_ref[...], after_ref[...], m, n_x)
        total = jnp.zeros((TILE, channels), F32)
        for d in range(3):
            left = pieces[2 - d].astype(F32).T.astype(BF)
            total += jnp.dot(left, w_ref[d], preferred_element_type=F32)
        emit_chunks(total, scratch, out_refs, c, n_ch, cb)

    *chunks, stack = pl.pallas_call(
        body,
        out_shape=chunk_shapes(n_ch, cb) + [jax.ShapeDtypeStruct((n_x, cb, TILE), BF)],
        scratch_shapes=[pltpu.VMEM((channels, TILE), F32)],
        compiler_params=pltpu.CompilerParams(vmem_limit_bytes=16 * MIB),
        cost_estimate=pl.CostEstimate(flops=2000000000, transcendentals=0, bytes_accessed=3_000_000),
        name="temporal_backward",
    )(*ring, weight)
    return chunks, stack


def shifted_columns(frame, toward):
    cells = frame.T
    col = lax.broadcasted_iota(jnp.int32, cells.shape, 0) % W
    out = []
    for dc in (-toward, 0, toward):
        moved = cells
        if dc:
            ok = (col + dc >= 0) & (col + dc < W)
            moved = jnp.where(ok, pltpu.roll(cells, (-dc) % FRAME, 0), 0.0)
        out.append(moved.astype(BF))
    return out


def spatial_backward(field, sibling, weight):
    n_ch, _ = sizes()
    cb = field.shape[0]
    channels = n_ch * cb

    def body(field_ref, sibling_ref, w_ref, *rest):
        out_refs, (left, scratch) = rest[:n_ch], rest[n_ch:]
        c, _, band = place()
        blank = jnp.zeros((W, 3 * cb), BF)
        for a, frame in enumerate(frames_of(field_ref[...], sibling_ref[...], band)):
            left[a, :W, :] = blank
            left[a, W + FRAME :, :] = blank
            for q, moved in enumerate(shifted_columns(frame, -1)):
                left[a, W : W + FRAME, q * cb : (q + 1) * cb] = moved
        total = jnp.zeros((TILE, channels), F32)
        for g in range(3):
            start = pl.multiple_of(HALF * band + W * (2 - g), W)
            rows = jnp.concatenate([left[a, pl.ds(start, HALF), :] for a in range(FT)], axis=0)
            total += jnp.dot(rows, w_ref[g], preferred_element_type=F32)
        emit_chunks(total, scratch, out_refs, c, n_ch, cb)

    return pl.pallas_call(
        body,
        out_shape=chunk_shapes(n_ch, cb),
        scratch_shapes=[
            pltpu.VMEM((FT, FRAME + 2 * W, 3 * cb), BF),
            pltpu.VMEM((channels, TILE), F32),
        ],
        compiler_params=pltpu.CompilerParams(vmem_limit_bytes=16 * MIB),
        name="spatial_backward",
    )(field, sibling, weight.reshape(3, 3 * cb, channels))


def spatial_grads(grads, grads_sibling, fields, fields_sibling, own_sum, partials, scale):
    _, n_x = sizes()
    ob, ib = grads[0].shape[0], fields[0].shape[0]
    frames = FT * n_x
    n_p = len(partials)

    def body(*refs):
        g_refs, gs_refs, l_refs, ls_refs = (refs[q * n_x : (q + 1) * n_x] for q in range(4))
        own_ref, partial_refs = refs[4 * n_x], refs[4 * n_x + 1 : 4 * n_x + 1 + n_p]
        out_hbm, latent_hbm, left, right, out, latent, sems = refs[4 * n_x + 1 + n_p :]
        total = g_refs[0][...].astype(F32) + own_ref[...]
        for partial_ref in partial_refs:
            total += partial_ref[...].astype(F32)
        latent[...] = total.astype(BF)
        latent_copy = pltpu.make_async_copy(latent, latent_hbm, sems.at[9])
        latent_copy.start()
        _, _, band = place()
        blank = jnp.zeros((W, ib), BF)
        for j in range(n_x):
            for a, frame in enumerate(frames_of(g_refs[j][...], gs_refs[j][...], band)):
                f = FT * j + a
                left[:, f * FRAME : (f + 1) * FRAME] = frame.astype(BF)
            for a, frame in enumerate(frames_of(l_refs[j][...], ls_refs[j][...], band)):
                f = FT * j + a
                for q, moved in enumerate(shifted_columns(frame, 1)):
                    right[q, f, :W, :] = blank
                    right[q, f, W + FRAME :, :] = blank
                    right[q, f, W : W + FRAME, :] = moved
        copies = []
        for tap in range(9):
            at = slice(W * (tap // 3), W * (tap // 3) + FRAME)
            moved = jnp.concatenate([right[tap % 3, f, at, :] for f in range(frames)], axis=0)
            out[tap] = jnp.dot(left[...], moved, preferred_element_type=F32) * scale
            copies.append(pltpu.make_async_copy(out.at[tap], out_hbm.at[tap], sems.at[tap]))
            copies[-1].start()
        for copy in copies:
            copy.wait()
        latent_copy.wait()

    return pl.pallas_call(
        body,
        out_specs=[pl.BlockSpec(memory_space=pltpu.HBM)] * 2,
        out_shape=[jax.ShapeDtypeStruct((9, ob, ib), F32), jax.ShapeDtypeStruct((ob, TILE), BF)],
        scratch_shapes=[
            pltpu.VMEM((ob, frames * FRAME), BF),
            pltpu.VMEM((3, frames, FRAME + 2 * W, ib), BF),
            pltpu.VMEM((9, ob, ib), F32),
            pltpu.VMEM((ob, TILE), BF),
            pltpu.SemaphoreType.DMA((10,)),
        ],
        compiler_params=pltpu.CompilerParams(vmem_limit_bytes=24 * MIB),
        name="spatial_grads",
    )(*grads, *grads_sibling, *fields, *fields_sibling, own_sum, *partials)


def temporal_grads(grads, grads_sibling, fields, fields_sibling, scale):
    _, n_x = sizes()
    ob, ib = grads.shape[1], fields[0].shape[0]
    span = FT * n_x * FRAME

    def body(*refs):
        g_ref, gs_ref = refs[:2]
        h_refs, hs_refs = refs[2 : 2 + n_x], refs[2 + n_x : 2 + 2 * n_x]
        out_hbm, left, right, out, sems = refs[2 + 2 * n_x :]
        _, m, band = place()
        right[:FRAME, :] = jnp.zeros((FRAME, ib), BF)
        right[FRAME + span :, :] = jnp.zeros((FRAME, ib), BF)
        for j in range(n_x):
            block = (m + n_x - j) % n_x
            for a, frame in enumerate(frames_of(g_ref[j], gs_ref[j], band)):
                at = pl.multiple_of((FT * block + a) * FRAME, FRAME)
                left[:, pl.ds(at, FRAME)] = frame.astype(BF)
            for a, frame in enumerate(frames_of(h_refs[j][...], hs_refs[j][...], band)):
                at = pl.multiple_of((FT * block + a + 1) * FRAME, FRAME)
                right[pl.ds(at, FRAME), :] = frame.T.astype(BF)
        copies = []
        for d in range(3):
            moved = right[d * FRAME : d * FRAME + span, :]
            out[d] = jnp.dot(left[...], moved, preferred_element_type=F32) * scale
            copies.append(pltpu.make_async_copy(out.at[d], out_hbm.at[d], sems.at[d]))
            copies[-1].start()
        for copy in copies:
            copy.wait()

    return pl.pallas_call(
        body,
        out_specs=pl.BlockSpec(memory_space=pltpu.HBM),
        out_shape=jax.ShapeDtypeStruct((3, ob, ib), F32),
        scratch_shapes=[
            pltpu.VMEM((ob, span), BF),
            pltpu.VMEM((span + 2 * FRAME, ib), BF),
            pltpu.VMEM((3, ob, ib), F32),
            pltpu.SemaphoreType.DMA((3,)),
        ],
        compiler_params=pltpu.CompilerParams(vmem_limit_bytes=24 * MIB),
        name="temporal_grads",
    )(grads, grads_sibling, *fields, *fields_sibling)


def scatter_ch(chunks):
    return [send(chunks[k], "ch", k) for k in range(1, len(chunks))]


def total_of(base, own, received):
    total = base.astype(F32) + own
    for chunk in received:
        total = total + chunk.astype(F32)
    return total.astype(BF)


def on_device(latents, spatial_weight, temporal_weight, cotangent):
    n_ch, n_x = sizes()
    assert n_ch == RBANDS * n_x
    c, m, band = place()
    scale = 1.0 / math.sqrt(TILE * RBANDS * n_x)

    def block(pieces, b):
        stack = jnp.stack(pieces) if isinstance(pieces, list) else pieces
        return lax.dynamic_index_in_dim(stack, (c + n_ch - b) % n_ch, 0, keepdims=False)

    own_block = RBANDS * m + band
    sib_block = RBANDS * m + 1 - band

    siblings = [swap_band(latents)]
    mine = gather_ch(latents)
    cot_ring = ring_blocks(cotangent)
    chunks, cots = temporal_backward([cotangent] + cot_ring, temporal_weight)
    partials = scatter_ch(chunks)
    mine = after_all(mine, chunks)

    siblings += [swap_band(piece) for piece in mine[1:]]
    cots_sibling = swap_band(cots)
    lat_own, lat_sib = [block(mine, own_block)], [block(siblings, own_block)]
    for j in range(1, n_x):
        target = RBANDS * ((m + j) % n_x) + band
        both = send(jnp.stack([block(mine, target), block(siblings, target)]), "st", RBANDS * j)
        lat_own.append(both[0])
        lat_sib.append(both[1])
    hidden = spatial_forward(mine, siblings, spatial_weight)
    hidden_mine = gather_ch(hidden)

    hidden_grad = total_of(after_all(cotangent, hidden), chunks[0], partials)
    grad_ring = ring_blocks(hidden_grad)
    grad_sibling = swap_band(hidden_grad)
    chunks = spatial_backward(hidden_grad, grad_sibling, spatial_weight)
    partials = scatter_ch(chunks)

    grads = [hidden_grad] + grad_ring
    grads_sibling = [grad_sibling] + [swap_band(x) for x in grad_ring]
    lat_own = after_all(lat_own, partials)
    spatial_grad, latent_grad = spatial_grads(
        grads, grads_sibling, lat_own, lat_sib, chunks[0], partials, scale
    )

    hidden_mine = after_all(hidden_mine, chunks)
    before, after = neighbours(jnp.stack(hidden_mine))
    before, after = after_all((before, after), spatial_grad)
    temporal_out = temporal_forward(hidden_mine, before, after, temporal_weight)

    hid_own, hid_sib = [block(hidden_mine, own_block)], [block(hidden_mine, sib_block)]
    for j in range(1, n_x):
        if n_x == 2:
            hid_own.append(block(before, own_block))
            hid_sib.append(block(before, sib_block))
        else:
            target = RBANDS * ((m + j) % n_x)
            both = jnp.stack([block(hidden_mine, target + band), block(hidden_mine, target + 1 - band)])
            both = send(both, "st", RBANDS * j)
            hid_own.append(both[0])
            hid_sib.append(both[1])
    temporal_grad = temporal_grads(cots, cots_sibling, hid_own, [swap_band(x) for x in hid_sib], scale)

    return temporal_out, latent_grad, spatial_grad, temporal_grad


def solution(mesh):
    return jax.shard_map(
        on_device,
        mesh=mesh,
        in_specs=(
            P("ch", ("groups", "st")),
            P(None, "ch", None),
            P(None, "ch", None),
            P("ch", ("groups", "st")),
        ),
        out_specs=(
            P("ch", ("groups", "st")),
            P("ch", ("groups", "st")),
            P("groups", "ch", "st"),
            P("groups", "ch", "st"),
        ),
        check_vma=False,
    )
```

```python
import math

import jax
import jax.numpy as jnp
from jax import lax
from jax.experimental import pallas as pl
from jax.experimental.pallas import tpu as pltpu
from jax.sharding import PartitionSpec as P

FT = 2
RT = 2
W = 32
RBANDS = 2
TILE = FT * RT * W
HALF = RT * W
ROWS = RBANDS * RT
FRAME = ROWS * W
MIB = 1 << 20
BF = jnp.bfloat16
F32 = jnp.float32


def sizes():
    return lax.axis_size("ch"), lax.axis_size("st") // RBANDS


def place():
    st = lax.axis_index("st")
    return lax.axis_index("ch"), st // RBANDS, st % RBANDS


def send(data, axis, by):
    n = lax.axis_size(axis)
    return lax.ppermute(data, axis, [(i, (i + by) % n) for i in range(n)])


def swap_band(data):
    n = lax.axis_size("st")
    return lax.ppermute(data, "st", [(i, i ^ 1) for i in range(n)])


def after_all(values, others):
    return lax.optimization_barrier((values, others))[0]


def gather_ch(shard):
    n_ch, _ = sizes()
    return [shard] + [send(shard, "ch", k) for k in range(1, n_ch)]


def ring_blocks(data):
    _, n_x = sizes()
    return [send(data, "st", RBANDS * j) for j in range(1, n_x)]


def neighbours(data):
    _, n_x = sizes()
    if n_x == 2:
        other = send(data, "st", RBANDS)
        return other, other
    return send(data, "st", RBANDS), send(data, "st", -RBANDS)


def lanes(shape):
    return lax.broadcasted_iota(jnp.int32, shape, len(shape) - 1)


def roll(x, by):
    return pltpu.roll(x, by, x.ndim - 1)


def frames_of(own, sibling, band):
    own = own.astype(F32)
    sibling = sibling.astype(F32)
    first = jnp.where(band == 0, own, sibling)
    second = jnp.where(band == 0, sibling, own)
    low = lanes(first.shape) < HALF
    crossed = roll(jnp.where(low, second, first), HALF)
    return jnp.where(low, first, crossed), jnp.where(low, crossed, second)


def tile_of(frame0, frame1, band):
    low = lanes(frame0.shape) < HALF
    moved = roll(jnp.where(band == 0, frame1, frame0), HALF)
    return jnp.where(band == 0, jnp.where(low, frame0, moved), jnp.where(low, moved, frame1))


def time_pieces(own, before, after, m, n_x):
    own32 = own.astype(F32)
    before = jnp.where(m > 0, before.astype(F32), 0.0)
    after = jnp.where(m < n_x - 1, after.astype(F32), 0.0)
    low = lanes(own32.shape) < HALF
    earlier = roll(jnp.where(low, own32, before), HALF)
    later = roll(jnp.where(low, after, own32), HALF)
    return earlier.astype(BF), own, later.astype(BF)


def inside(dr, dc, shape):
    lane = lanes(shape)
    row = lane // W + dr
    col = lane % W + dc
    return (row >= 0) & (row < ROWS) & (col >= 0) & (col < W)


def spatial_forward(mine, siblings, weight):
    n_ch, n_x = sizes()
    cb = mine[0].shape[0]
    channels = n_ch * cb

    def body(*refs):
        mine_refs, sibling_refs = refs[:n_ch], refs[n_ch : 2 * n_ch]
        w_ref, out_ref, field, acc = refs[2 * n_ch :]
        c, _, band = place()
        for k in range(n_ch):
            at = pl.ds(pl.multiple_of(((c + n_ch - k) % n_ch) * cb, 16), cb)
            f0, f1 = frames_of(mine_refs[k][...], sibling_refs[k][...], band)
            field[at, :FRAME] = f0.astype(BF)
            field[at, FRAME:] = f1.astype(BF)
        for tap in range(9):
            dr, dc = tap // 3 - 1, tap % 3 - 1
            part = jnp.dot(w_ref[tap], field[...], preferred_element_type=F32)
            by = (-(W * dr + dc)) % FRAME
            ok = inside(dr, dc, (cb, FRAME))
            for a in range(FT):
                at = slice(a * FRAME, (a + 1) * FRAME)
                moved = part[:, at]
                if by:
                    moved = jnp.where(ok, roll(moved, by), 0.0)
                acc[:, at] = moved + acc[:, at] if tap else moved
        total = tile_of(acc[:, :FRAME], acc[:, FRAME:], band)
        out_ref[...] = (mine_refs[0][...].astype(F32) + total).astype(BF)

    return pl.pallas_call(
        body,
        out_shape=jax.ShapeDtypeStruct((cb, TILE), BF),
        scratch_shapes=[pltpu.VMEM((channels, FT * FRAME), BF), pltpu.VMEM((cb, FT * FRAME), F32)],
        compiler_params=pltpu.CompilerParams(vmem_limit_bytes=16 * MIB),
        name="spatial_forward",
    )(*mine, *siblings, weight)


def temporal_forward(mine, before, after, weight):
    n_ch, n_x = sizes()
    cb = mine[0].shape[0]
    channels = n_ch * cb

    def body(*refs):
        mine_refs = refs[:n_ch]
        before_ref, after_ref, w_ref, out_ref, field = refs[n_ch:]
        c, m, _ = place()
        for k in range(n_ch):
            at = pl.ds(pl.multiple_of(((c + n_ch - k) % n_ch) * cb, 16), cb)
            pieces = time_pieces(mine_refs[k][...], before_ref[k], after_ref[k], m, n_x)
            for d in range(3):
                field[d, at, :] = pieces[d]
        total = mine_refs[0][...].astype(F32)
        for d in range(3):
            total += jnp.dot(w_ref[d], field[d], preferred_element_type=F32)
        out_ref[...] = total.astype(BF)

    return pl.pallas_call(
        body,
        out_shape=jax.ShapeDtypeStruct((cb, TILE), BF),
        scratch_shapes=[pltpu.VMEM((3, channels, TILE), BF)],
        compiler_params=pltpu.CompilerParams(vmem_limit_bytes=16 * MIB),
        name="temporal_forward",
    )(*mine, before, after, weight)


def emit_chunks(total, scratch, out_refs, c, n_ch, cb):
    scratch[...] = total.T
    for k in range(n_ch):
        at = pl.ds(pl.multiple_of(((c + k) % n_ch) * cb, 16), cb)
        out_refs[k][...] = scratch[at, :].astype(out_refs[k].dtype)


def chunk_shapes(n_ch, cb):
    return [jax.ShapeDtypeStruct((cb, TILE), BF if k else F32) for k in range(n_ch)]


def temporal_backward(ring, weight):
    n_ch, n_x = sizes()
    field = ring[0]
    cb = field.shape[0]
    channels = n_ch * cb

    def body(*refs):
        ring_refs, w_ref, out_refs = refs[:n_x], refs[n_x], refs[n_x + 1 : n_x + 1 + n_ch]
        stack_ref, scratch = refs[n_x + 1 + n_ch :]
        field_ref, before_ref, after_ref = ring_refs[0], ring_refs[1], ring_refs[-1]
        c, m, _ = place()
        for j in range(n_x):
            stack_ref[j] = ring_refs[j][...]
        pieces = time_pieces(field_ref[...], before_ref[...], after_ref[...], m, n_x)
        total = jnp.zeros((TILE, channels), F32)
        for d in range(3):
            left = pieces[2 - d].astype(F32).T.astype(BF)
            total += jnp.dot(left, w_ref[d], preferred_element_type=F32)
        emit_chunks(total, scratch, out_refs, c, n_ch, cb)

    *chunks, stack = pl.pallas_call(
        body,
        out_shape=chunk_shapes(n_ch, cb) + [jax.ShapeDtypeStruct((n_x, cb, TILE), BF)],
        scratch_shapes=[pltpu.VMEM((channels, TILE), F32)],
        compiler_params=pltpu.CompilerParams(vmem_limit_bytes=16 * MIB),
        cost_estimate=pl.CostEstimate(flops=2000000000, transcendentals=0, bytes_accessed=3_000_000),
        name="temporal_backward",
    )(*ring, weight)
    return chunks, stack


def shifted_columns(frame, toward):
    cells = frame.T
    col = lax.broadcasted_iota(jnp.int32, cells.shape, 0) % W
    out = []
    for dc in (-toward, 0, toward):
        moved = cells
        if dc:
            ok = (col + dc >= 0) & (col + dc < W)
            moved = jnp.where(ok, pltpu.roll(cells, (-dc) % FRAME, 0), 0.0)
        out.append(moved.astype(BF))
    return out


def spatial_backward(field, sibling, weight):
    n_ch, _ = sizes()
    cb = field.shape[0]
    channels = n_ch * cb

    def body(field_ref, sibling_ref, w_ref, *rest):
        out_refs, (left, scratch) = rest[:n_ch], rest[n_ch:]
        c, _, band = place()
        blank = jnp.zeros((W, 3 * cb), BF)
        for a, frame in enumerate(frames_of(field_ref[...], sibling_ref[...], band)):
            left[a, :W, :] = blank
            left[a, W + FRAME :, :] = blank
            for q, moved in enumerate(shifted_columns(frame, -1)):
                left[a, W : W + FRAME, q * cb : (q + 1) * cb] = moved
        total = jnp.zeros((TILE, channels), F32)
        for g in range(3):
            start = pl.multiple_of(HALF * band + W * (2 - g), W)
            rows = jnp.concatenate([left[a, pl.ds(start, HALF), :] for a in range(FT)], axis=0)
            total += jnp.dot(rows, w_ref[g], preferred_element_type=F32)
        emit_chunks(total, scratch, out_refs, c, n_ch, cb)

    return pl.pallas_call(
        body,
        out_shape=chunk_shapes(n_ch, cb),
        scratch_shapes=[
            pltpu.VMEM((FT, FRAME + 2 * W, 3 * cb), BF),
            pltpu.VMEM((channels, TILE), F32),
        ],
        compiler_params=pltpu.CompilerParams(vmem_limit_bytes=16 * MIB),
        name="spatial_backward",
    )(field, sibling, weight.reshape(3, 3 * cb, channels))


def spatial_grads(grads, grads_sibling, fields, fields_sibling, own_sum, partials, scale):
    _, n_x = sizes()
    ob, ib = grads[0].shape[0], fields[0].shape[0]
    frames = FT * n_x
    n_p = len(partials)

    def body(*refs):
        g_refs, gs_refs, l_refs, ls_refs = (refs[q * n_x : (q + 1) * n_x] for q in range(4))
        own_ref, partial_refs = refs[4 * n_x], refs[4 * n_x + 1 : 4 * n_x + 1 + n_p]
        out_hbm, latent_hbm, left, right, out, latent, sems = refs[4 * n_x + 1 + n_p :]
        total = g_refs[0][...].astype(F32) + own_ref[...]
        for partial_ref in partial_refs:
            total += partial_ref[...].astype(F32)
        latent[...] = total.astype(BF)
        latent_copy = pltpu.make_async_copy(latent, latent_hbm, sems.at[9])
        latent_copy.start()
        _, _, band = place()
        blank = jnp.zeros((W, ib), BF)
        for j in range(n_x):
            for a, frame in enumerate(frames_of(g_refs[j][...], gs_refs[j][...], band)):
                f = FT * j + a
                left[:, f * FRAME : (f + 1) * FRAME] = frame.astype(BF)
            for a, frame in enumerate(frames_of(l_refs[j][...], ls_refs[j][...], band)):
                f = FT * j + a
                for q, moved in enumerate(shifted_columns(frame, 1)):
                    right[q, f, :W, :] = blank
                    right[q, f, W + FRAME :, :] = blank
                    right[q, f, W : W + FRAME, :] = moved
        copies = []
        for tap in range(9):
            at = slice(W * (tap // 3), W * (tap // 3) + FRAME)
            moved = jnp.concatenate([right[tap % 3, f, at, :] for f in range(frames)], axis=0)
            out[tap] = jnp.dot(left[...], moved, preferred_element_type=F32) * scale
            copies.append(pltpu.make_async_copy(out.at[tap], out_hbm.at[tap], sems.at[tap]))
            copies[-1].start()
        for copy in copies:
            copy.wait()
        latent_copy.wait()

    return pl.pallas_call(
        body,
        out_specs=[pl.BlockSpec(memory_space=pltpu.HBM)] * 2,
        out_shape=[jax.ShapeDtypeStruct((9, ob, ib), F32), jax.ShapeDtypeStruct((ob, TILE), BF)],
        scratch_shapes=[
            pltpu.VMEM((ob, frames * FRAME), BF),
            pltpu.VMEM((3, frames, FRAME + 2 * W, ib), BF),
            pltpu.VMEM((9, ob, ib), F32),
            pltpu.VMEM((ob, TILE), BF),
            pltpu.SemaphoreType.DMA((10,)),
        ],
        compiler_params=pltpu.CompilerParams(vmem_limit_bytes=24 * MIB),
        name="spatial_grads",
    )(*grads, *grads_sibling, *fields, *fields_sibling, own_sum, *partials)


def temporal_grads(grads, grads_sibling, fields, fields_sibling, scale):
    _, n_x = sizes()
    ob, ib = grads.shape[1], fields[0].shape[0]
    span = FT * n_x * FRAME

    def body(*refs):
        g_ref, gs_ref = refs[:2]
        h_refs, hs_refs = refs[2 : 2 + n_x], refs[2 + n_x : 2 + 2 * n_x]
        out_hbm, left, right, out, sems = refs[2 + 2 * n_x :]
        _, m, band = place()
        right[:FRAME, :] = jnp.zeros((FRAME, ib), BF)
        right[FRAME + span :, :] = jnp.zeros((FRAME, ib), BF)
        for j in range(n_x):
            block = (m + n_x - j) % n_x
            for a, frame in enumerate(frames_of(g_ref[j], gs_ref[j], band)):
                at = pl.multiple_of((FT * block + a) * FRAME, FRAME)
                left[:, pl.ds(at, FRAME)] = frame.astype(BF)
            for a, frame in enumerate(frames_of(h_refs[j][...], hs_refs[j][...], band)):
                at = pl.multiple_of((FT * block + a + 1) * FRAME, FRAME)
                right[pl.ds(at, FRAME), :] = frame.T.astype(BF)
        copies = []
        for d in range(3):
            moved = right[d * FRAME : d * FRAME + span, :]
            out[d] = jnp.dot(left[...], moved, preferred_element_type=F32) * scale
            copies.append(pltpu.make_async_copy(out.at[d], out_hbm.at[d], sems.at[d]))
            copies[-1].start()
        for copy in copies:
            copy.wait()

    return pl.pallas_call(
        body,
        out_specs=pl.BlockSpec(memory_space=pltpu.HBM),
        out_shape=jax.ShapeDtypeStruct((3, ob, ib), F32),
        scratch_shapes=[
            pltpu.VMEM((ob, span), BF),
            pltpu.VMEM((span + 2 * FRAME, ib), BF),
            pltpu.VMEM((3, ob, ib), F32),
            pltpu.SemaphoreType.DMA((3,)),
        ],
        compiler_params=pltpu.CompilerParams(vmem_limit_bytes=24 * MIB),
        name="temporal_grads",
    )(grads, grads_sibling, *fields, *fields_sibling)


def scatter_ch(chunks):
    return [send(chunks[k], "ch", k) for k in range(1, len(chunks))]


def total_of(base, own, received):
    total = base.astype(F32) + own
    for chunk in received:
        total = total + chunk.astype(F32)
    return total.astype(BF)


def on_device(latents, spatial_weight, temporal_weight, cotangent):
    n_ch, n_x = sizes()
    assert n_ch == RBANDS * n_x
    c, m, band = place()
    scale = 1.0 / math.sqrt(TILE * RBANDS * n_x)

    def block(pieces, b):
        stack = jnp.stack(pieces) if isinstance(pieces, list) else pieces
        return lax.dynamic_index_in_dim(stack, (c + n_ch - b) % n_ch, 0, keepdims=False)

    own_block = RBANDS * m + band
    sib_block = RBANDS * m + 1 - band

    siblings = [swap_band(latents)]
    mine = gather_ch(latents)
    cot_ring = ring_blocks(cotangent)
    chunks, cots = temporal_backward([cotangent] + cot_ring, temporal_weight)
    partials = scatter_ch(chunks)
    mine = after_all(mine, chunks)

    siblings += [swap_band(piece) for piece in mine[1:]]
    cots_sibling = swap_band(cots)
    lat_own, lat_sib = [block(mine, own_block)], [block(siblings, own_block)]
    for j in range(1, n_x):
        target = RBANDS * ((m + j) % n_x) + band
        both = send(jnp.stack([block(mine, target), block(siblings, target)]), "st", RBANDS * j)
        lat_own.append(both[0])
        lat_sib.append(both[1])
    hidden = spatial_forward(mine, siblings, spatial_weight)
    hidden_mine = gather_ch(hidden)

    hidden_grad = total_of(after_all(cotangent, hidden), chunks[0], partials)
    grad_ring = ring_blocks(hidden_grad)
    grad_sibling = swap_band(hidden_grad)
    chunks = spatial_backward(hidden_grad, grad_sibling, spatial_weight)
    partials = scatter_ch(chunks)

    grads = [hidden_grad] + grad_ring
    grads_sibling = [grad_sibling] + [swap_band(x) for x in grad_ring]
    lat_own = after_all(lat_own, partials)
    spatial_grad, latent_grad = spatial_grads(
        grads, grads_sibling, lat_own, lat_sib, chunks[0], partials, scale
    )

    hidden_mine = after_all(hidden_mine, chunks)
    before, after = neighbours(jnp.stack(hidden_mine))
    before, after = after_all((before, after), spatial_grad)
    temporal_out = temporal_forward(hidden_mine, before, after, temporal_weight)

    hid_own, hid_sib = [block(hidden_mine, own_block)], [block(hidden_mine, sib_block)]
    for j in range(1, n_x):
        if n_x == 2:
            hid_own.append(block(before, own_block))
            hid_sib.append(block(before, sib_block))
        else:
            target = RBANDS * ((m + j) % n_x)
            both = jnp.stack([block(hidden_mine, target + band), block(hidden_mine, target + 1 - band)])
            both = send(both, "st", RBANDS * j)
            hid_own.append(both[0])
            hid_sib.append(both[1])
    temporal_grad = temporal_grads(cots, cots_sibling, hid_own, [swap_band(x) for x in hid_sib], scale)

    return temporal_out, latent_grad, spatial_grad, temporal_grad


def solution(mesh):
    return jax.shard_map(
        on_device,
        mesh=mesh,
        in_specs=(
            P("ch", ("groups", "st")),
            P(None, "ch", None),
            P(None, "ch", None),
            P("ch", ("groups", "st")),
        ),
        out_specs=(
            P("ch", ("groups", "st")),
            P("ch", ("groups", "st")),
            P("groups", "ch", "st"),
            P("groups", "ch", "st"),
        ),
        check_vma=False,
    )
```
